1024 devices in a mesh: blk: 16 (over y_hi, x), group: 64 (over z, y_lo, core).
Axes of the slice: x: 8, y: 8 (y_hi: 2, y_lo: 4; y = y_hi * 4 + y_lo), z: 8, core: 2. Of those that a mesh axis runs over, the one named last changes fastest.
Arguments:
- star_pos: float32 [3, 131072], P(None, 'blk'), may hold values from -6 to 6
- star_vel: float32 [3, 131072], P(None, 'blk'), may hold values from -6 to 6
- star_acc: float32 [3, 131072], P(None, 'blk'), may hold values from -6 to 6
- star_jerk: float32 [3, 131072], P(None, 'blk'), may hold values from -6 to 6
- star_mass: float32 [131072], P('blk'), may hold values from 0.25 to 4
- star_dt: float32 [131072], P('blk'), may hold values from 0.0625 to 1
- active_list: int32 [16, 64, 128], P('blk', 'group'), may hold values from 0 to 8191
- active_count: int32 [16, 64], P('blk', 'group'), may hold values from 1 to 128, 2048 in all within a row
Outputs:
- accel_jerk: float32 [16, 64, 6, 128], P('blk', 'group')
The draws below stay inside these ranges and needn't reach their ends.
Inputs may be any that keep to these rules, and one draw needn't show every extreme that they name: `active_list`: only the first active_count slots of a list are active, the rest are ignored; entries may repeat. `active_count`: for each blk index the counts over group sum to 2048, and one of them is exactly 128.
All inputs are finite; a program needn't handle non-finite values.
Results may differ from the reference program's by a relative error of at most 0.00012.
Values sent between devices are 32-bit elements; how exact they have to be, the bound alone decides.
A program may use at most 32 MiB of HBM per device.

```python
import math
import jax
import jax.numpy as jnp
import numpy as np
from jax import lax

STAR_DEV = 8192
ACT_AVG = 32
ACT_MAX = 128
N_STAR = 131072
N_BLK = 16
N_GROUP = 64


def plant(values, key, low, largest):
    dims = values.shape
    index_at = [jax.random.randint(jax.random.fold_in(key, axis), (), 0, dims[axis]) for axis in range(len(dims))]
    values = values.at[tuple(index_at)].set(low)
    longest = dims.index(max(dims))
    index_at[longest] = (index_at[longest] + 1) % dims[longest]
    return values.at[tuple(index_at)].set(largest)


def block_scale(stream_key, shape, pieces, least, high):
    factor_of, own = 1.0, jax.random.fold_in(stream_key, 6)
    for position, blocks in pieces:
        heights = jnp.exp(jax.random.uniform(jax.random.fold_in(own, position), (blocks,), jnp.float32, least / len(pieces), high / len(pieces)))
        factor_of = factor_of * jnp.repeat(heights, shape[position] // blocks).reshape([-1 if axis == position else 1 for axis in range(len(shape))])
    return factor_of


def rank_bounds(amount, skew):
    weights = [(1 << 20) // math.isqrt(standing ** skew) + 1 for standing in range(1, amount + 1)]
    scale = 1 + sum(weights) // (1 << 30)
    return np.cumsum(np.array([max(1, weight // scale) for weight in weights]))


def skewed_ids(stream_key, dims, amount, skew):
    grid = rank_bounds(amount, skew)
    ticket = jax.random.randint(jax.random.fold_in(stream_key, 1), dims, 0, int(grid[amount - 1]))
    rank = jnp.searchsorted(jnp.asarray(grid, jnp.int32), ticket, side="right")
    return jax.random.permutation(jax.random.fold_in(stream_key, 2), amount)[rank].astype(jnp.int32)


def split_up(number_of, total, most, slope):
    portions = [(1 << 20) // math.isqrt(grade ** slope) + 1 for grade in range(2, number_of + 1)]
    spare, counts = total - most - (number_of - 1), [1] * (number_of - 1)
    while spare > 0:
        candidates = [i for i in range(number_of - 1) if counts[i] < most]
        mass, remaining = sum([portions[i] for i in candidates]), spare
        for i in candidates:
            extra = min(most - counts[i], max(1, remaining * portions[i] // mass), spare)
            counts[i] = counts[i] + extra
            spare = spare - extra
    return np.array([most] + counts)


def uneven(own_key, count, total, limit, skew):
    if count == 2:
        one = jax.random.randint(own_key, (), max(1, total - limit), min(limit, total - 1) + 1)
        return jnp.stack([one, total - one])
    tallies = jnp.asarray(split_up(count, total, limit, skew), jnp.int32)
    couples = (count - 1) // 2
    source_of, receiver = tallies[1:1 + 2 * couples:2], tallies[2:2 + 2 * couples:2]
    room = jnp.minimum(source_of - 1, limit - receiver)
    shifted = jax.random.randint(jax.random.fold_in(own_key, 1), (couples,), 0, 1 << 20) % (room + 1)
    tallies = tallies.at[1:1 + 2 * couples:2].set(source_of - shifted).at[2:2 + 2 * couples:2].set(receiver + shifted)
    return tallies[jax.random.permutation(jax.random.fold_in(own_key, 2), count)]


def scatter_about(rng, extent, spread, reach, split=(), kind=jnp.bfloat16):
    drawn = spread * jax.random.normal(rng, extent, jnp.float32)
    if split:
        drawn = drawn * block_scale(rng, extent, split, -0.22, 0.18)
    return jnp.clip(drawn, -reach, reach).astype(kind)


def setup_inputs(seed: int = 0) -> dict:
    key_list = jax.random.split(jax.random.key(seed), 9)
    star_pos = scatter_about(key_list[0], (3, N_STAR), 1.0, 6.0, ((1, 16),), jnp.float32)
    star_vel = scatter_about(key_list[1], (3, N_STAR), 0.5, 6.0, ((1, 16),), jnp.float32)
    star_acc = scatter_about(key_list[2], (3, N_STAR), 1.0, 6.0, ((1, 16),), jnp.float32)
    star_jerk = scatter_about(key_list[3], (3, N_STAR), 2.0, 6.0, ((1, 16),), jnp.float32)
    star_mass = jnp.clip(jnp.exp(math.log(4.0) - 2.7725887 * jax.random.uniform(key_list[4], (N_STAR,), jnp.float32) ** block_scale(key_list[4], (N_STAR,), ((0, 16),), -0.2, 0.2)), 0.25, 4.0)
    star_dt = jnp.clip(jnp.exp(math.log(1.0) - 2.7725887 * jax.random.uniform(key_list[5], (N_STAR,), jnp.float32) ** block_scale(key_list[5], (N_STAR,), ((0, 16),), -0.2, 0.2)), 0.0625, 1.0)
    active_list = plant(skewed_ids(key_list[6], (N_BLK, N_GROUP, ACT_MAX), STAR_DEV, 2), jax.random.fold_in(key_list[6], 3), 0, STAR_DEV - 1).astype(jnp.int32)
    active_count = jax.vmap(lambda own: uneven(own, N_GROUP, ACT_AVG * N_GROUP, ACT_MAX, 2))(jax.random.split(key_list[7], N_BLK)).reshape((N_BLK, N_GROUP)).astype(jnp.int32)
    return dict(star_pos=star_pos, star_vel=star_vel, star_acc=star_acc, star_jerk=star_jerk, star_mass=star_mass, star_dt=star_dt, active_list=active_list, active_count=active_count)


soften = 0.01

def predict(pos, vel, acc, jerk, delta):
    step = delta[None, :]
    ppos = pos + step * (vel + step * (0.5 * acc + step * (jerk / 6.0)))
    pvel = vel + step * (acc + step * (0.5 * jerk))
    return (ppos, pvel)

def pair_block(rows, stars):
    gap = stars[0:3, None, :] - rows[0:3, :, None]
    drift = stars[3:6, None, :] - rows[3:6, :, None]
    inverse = lax.rsqrt(lax.optimization_barrier(jnp.sum(gap * gap, 0)) + soften)
    cube = stars[6][None, :] * inverse * inverse * inverse
    radial = 3.0 * lax.optimization_barrier(jnp.sum(gap * drift, 0)) * inverse * inverse
    accel = lax.optimization_barrier(jnp.sum(gap * cube[None], 2))
    jerks = lax.optimization_barrier(jnp.sum((drift - radial[None] * gap) * cube[None], 2))
    return jnp.concatenate([accel, jerks], 0)

def pair_sum(rows, stars):
    count = stars.shape[1]
    tile_size = max(128, 262144 // rows.shape[1])
    if count > tile_size and count % tile_size == 0:

        def advance(total, index):
            piece = lax.dynamic_slice_in_dim(stars, index * tile_size, tile_size, 1)
            return (total + pair_block(rows, piece), None)
        total, _ = lax.scan(advance, jnp.zeros((6, rows.shape[1]), jnp.float32), jnp.arange(count // tile_size))
        return total
    return pair_block(rows, stars)

def reference(star_pos, star_vel, star_acc, star_jerk, star_mass, star_dt, active_list, active_count):
    ppos, pvel = predict(star_pos, star_vel, star_acc, star_jerk, star_dt)
    weight = star_mass / N_STAR
    stars = jnp.concatenate([ppos, pvel, weight[None, :]], 0)
    offsets = (jnp.arange(N_BLK, dtype=jnp.int32) * STAR_DEV)[:, None, None]
    global_index = (active_list + offsets).reshape(-1).astype(jnp.int32)
    rows = jnp.take(jnp.concatenate([ppos, pvel], 0), global_index, axis=1)
    blocks = global_index.shape[0] // 1024

    def one_block(index):
        piece = lax.dynamic_slice_in_dim(rows, index * 1024, 1024, 1)
        return pair_sum(piece, stars)
    result = lax.map(one_block, jnp.arange(blocks))
    result = jnp.moveaxis(result, 0, 1).reshape(6, N_BLK, N_GROUP, ACT_MAX)
    result = jnp.transpose(result, (1, 2, 0, 3))
    live = jnp.arange(ACT_MAX, dtype=jnp.int32)[None, None, None, :] < active_count[:, :, None, None]
    return jnp.where(live, result, jnp.zeros_like(result))
```

```python
import functools

import jax
import jax.numpy as jnp
from jax import lax
from jax.experimental import pallas as pl
from jax.experimental.pallas import tpu as pltpu
from jax.sharding import PartitionSpec as P

MESH = pl.DeviceIdType.MESH
soften = 0.01
ROWS = 32
LANES = 128
HIGH = lax.Precision.HIGHEST


def pick(index, table):
    value = jnp.int32(table[-1])
    for place in range(len(table) - 2, -1, -1):
        value = jnp.where(index == place, jnp.int32(table[place]), value)
    return value


def chunk_order(high, low):
    def hops(item):
        return 4 * (item[0] % 2) + min(item[1], low - item[1])

    every = sorted([(h, l) for h in range(high) for l in range(low)], key=hops)
    first, rest = every[:3], every[3:]
    return first + rest[::-1]


def kernel(
    dims,
    pos_ref,
    vel_ref,
    acc_ref,
    jerk_ref,
    mass_ref,
    dt_ref,
    list_ref,
    count_ref,
    out_ref,
    tab,
    wide,
    near,
    lists,
    rows,
    res,
    part,
    tiles,
    strip,
    a_send,
    a_recv,
    b_send,
    b_recv,
    r_send,
    r_recv,
    p_send,
    p_recv,
    f_send,
    f_recv,
    g_send,
    g_recv,
):
    n_blk, low, n_far, n_near, total_stars = dims
    high = n_blk // low
    stars = mass_ref.shape[1]
    n_group = n_far * n_near
    order = chunk_order(high, low)
    order_high, order_low = [o[0] for o in order], [o[1] for o in order]
    b = lax.axis_index("blk")
    g = lax.axis_index("group")
    far = g // n_near
    close = lax.rem(g, n_near)

    def far_peer(step):
        return lax.rem(far + step, n_far)

    def near_peer(step):
        return lax.rem(close + step, n_near)

    def blk_peer(place):
        row = lax.rem(b // low + pick(place, order_high), high)
        column = lax.rem(lax.rem(b, low) + pick(place, order_low), low)
        return row * low + column

    barrier = pltpu.get_barrier_semaphore()
    for step in range(1, n_far):
        pl.semaphore_signal(
            barrier, 1, device_id={"group": far_peer(step) * n_near + close}, device_id_type=MESH
        )
    for step in range(1, n_near):
        pl.semaphore_signal(
            barrier, 1, device_id={"group": far * n_near + near_peer(step)}, device_id_type=MESH
        )
    for step in range(1, n_blk):
        pl.semaphore_signal(
            barrier, 1, device_id={"blk": lax.rem(b + step, n_blk)}, device_id_type=MESH
        )

    width = min(1024, stars)

    def predict(index, carry):
        here = pl.ds(pl.multiple_of(index * width, width), width)
        step = dt_ref[:, here]
        vel, acc, jerk = vel_ref[:, here], acc_ref[:, here], jerk_ref[:, here]
        ppos = pos_ref[:, here] + step * (vel + step * (0.5 * acc + step * (jerk / 6.0)))
        pvel = vel + step * (acc + step * (0.5 * jerk))
        weight = mass_ref[:, here] / total_stars
        tab[0:3, here] = ppos
        tab[3:6, here] = pvel
        tab[6:7, here] = weight
        tab[7:8, here] = jnp.zeros_like(weight)
        for row in range(3):
            wide[row, :, here] = jnp.broadcast_to(ppos[row : row + 1], (8, width))
            wide[3 + row, :, here] = jnp.broadcast_to(pvel[row : row + 1], (8, width))
        wide[6, :, here] = jnp.broadcast_to(weight, (8, width))
        return carry

    lax.fori_loop(0, stars // width, predict, 0)

    count = count_ref[0, 0]
    lane = lax.broadcasted_iota(jnp.int32, (1, LANES), 1)
    near[far] = jnp.where(lane < count, list_ref[...], -1)

    pl.semaphore_wait(barrier, (n_far - 1) + (n_near - 1) + (n_blk - 1))

    def a_copy(step, origin):
        return pltpu.make_async_remote_copy(
            src_ref=near.at[origin],
            dst_ref=near.at[origin],
            send_sem=a_send.at[step],
            recv_sem=a_recv.at[step],
            device_id={"group": far_peer(step) * n_near + close},
            device_id_type=MESH,
        )

    def b_copy(step, origin):
        return pltpu.make_async_remote_copy(
            src_ref=near,
            dst_ref=lists.at[origin],
            send_sem=b_send.at[step],
            recv_sem=b_recv.at[step],
            device_id={"group": far * n_near + near_peer(step)},
            device_id_type=MESH,
        )

    for step in range(1, n_far):
        a_copy(step, far).start()
    for step in range(1, n_far):
        a_copy(step, lax.rem(far + n_far - step, n_far)).wait_recv()
    for step in range(1, n_near):
        b_copy(step, close).start()
    lists[close] = near[...]
    for step in range(1, n_near):
        b_copy(step, lax.rem(close + n_near - step, n_near)).wait_recv()

    entry = lists[...].reshape(n_group, LANES)
    valid = entry >= 0
    validf = jnp.where(valid, 1.0, 0.0).astype(jnp.float32)
    entryf = entry.astype(jnp.float32)
    r_iota = lax.broadcasted_iota(jnp.int32, (n_group, n_group), 0)
    c_iota = lax.broadcasted_iota(jnp.int32, (n_group, n_group), 1)
    before = jnp.where(c_iota < r_iota, 1.0, 0.0).astype(jnp.float32)
    starts = jnp.sum(
        jnp.dot(before, validf, preferred_element_type=jnp.float32), axis=1, keepdims=True
    )
    slot = lax.broadcasted_iota(jnp.int32, (n_group, LANES), 1).astype(jnp.float32)
    base = (g * ROWS).astype(jnp.float32)
    place = jnp.where(valid, starts + slot - base, -1.0)
    mine = close * n_far + far
    owner_row = lax.broadcasted_iota(jnp.int32, (n_group, LANES), 0)
    my_start = jnp.sum(
        jnp.sum(jnp.where(owner_row < mine, validf, 0.0), axis=1, keepdims=True),
        axis=0,
        keepdims=True,
    )
    found = jnp.concatenate(
        [
            jnp.sum(jnp.where(place == float(s), entryf, 0.0), axis=0, keepdims=True)
            for s in range(ROWS)
        ],
        axis=0,
    )
    chosen = jnp.sum(found, axis=1, keepdims=True).astype(jnp.int32)
    column = lax.broadcasted_iota(jnp.int32, (ROWS, width), 1)

    def gather(index, total):
        here = pl.ds(pl.multiple_of(index * width, width), width)
        hot = jnp.where(column + index * width == chosen, 1.0, 0.0).astype(jnp.float32)
        return total + lax.dot_general(
            tab[:, here],
            hot,
            (((1,), (1,)), ((), ())),
            precision=HIGH,
            preferred_element_type=jnp.float32,
        )

    picked = lax.fori_loop(0, stars // width, gather, jnp.zeros((8, ROWS), jnp.float32))
    rows[b] = jnp.concatenate([picked, jnp.zeros((8, LANES - ROWS), jnp.float32)], axis=1)

    def r_copy(peer, origin):
        return pltpu.make_async_remote_copy(
            src_ref=rows.at[origin],
            dst_ref=rows.at[origin],
            send_sem=r_send.at[peer],
            recv_sem=r_recv.at[origin],
            device_id={"blk": peer},
            device_id_type=MESH,
        )

    def p_copy(peer, origin):
        return pltpu.make_async_remote_copy(
            src_ref=res.at[peer],
            dst_ref=part.at[origin],
            send_sem=p_send.at[peer],
            recv_sem=p_recv.at[origin],
            device_id={"blk": peer},
            device_id_type=MESH,
        )

    def send_rows(index, carry):
        r_copy(blk_peer(index), b).start()
        return carry

    lax.fori_loop(1, n_blk, send_rows, 0)

    half = 16
    out_lane = lax.broadcasted_iota(jnp.int32, (half, LANES), 1)

    def pairs(index, carry):
        peer = blk_peer(index)

        @pl.when(index > 0)
        def _():
            r_copy(peer, peer).wait_recv()

        across = jnp.transpose(rows[peer])
        pieces = []
        for top in range(0, ROWS, half):
            own = [
                jnp.broadcast_to(across[top : top + half, c : c + 1], (half, LANES))
                for c in range(6)
            ]

            def advance(tile, sums):
                here = pl.ds(pl.multiple_of(tile * LANES, LANES), LANES)
                star = [
                    jnp.concatenate([wide[c, :, here]] * (half // 8), axis=0) for c in range(7)
                ]
                rx, ry, rz = (star[c] - own[c] for c in range(3))
                ux, uy, uz = (star[3 + c] - own[3 + c] for c in range(3))
                inverse = lax.rsqrt((rx * rx + ry * ry) + (rz * rz + soften))
                square = inverse * inverse
                cube = (star[6] * inverse) * square
                radial = (3.0 * square) * (rx * ux + ry * uy + rz * uz)
                return (
                    sums[0] + cube * rx,
                    sums[1] + cube * ry,
                    sums[2] + cube * rz,
                    sums[3] + cube * (ux - radial * rx),
                    sums[4] + cube * (uy - radial * ry),
                    sums[5] + cube * (uz - radial * rz),
                )

            zero = jnp.zeros((half, LANES), jnp.float32)
            sums = lax.fori_loop(0, stars // LANES, advance, (zero,) * 6, unroll=4)
            piece = zero
            for c in range(6):
                piece = jnp.where(out_lane == c, jnp.sum(sums[c], axis=1, keepdims=True), piece)
            pieces.append(piece)
        pieces.append(jnp.zeros((LANES - ROWS, LANES), jnp.float32))
        result = jnp.transpose(jnp.concatenate(pieces, axis=0))[0:8]

        @pl.when(index == 0)
        def _():
            part[b] = result

        @pl.when(index > 0)
        def _():
            res[peer] = result
            p_copy(peer, b).start()

        return carry

    lax.fori_loop(0, n_blk, pairs, 0)

    def take_parts(index, carry):
        peer = blk_peer(index)
        p_copy(peer, peer).wait_recv()
        return carry

    lax.fori_loop(1, n_blk, take_parts, 0)
    force = jnp.sum(part[...], axis=0)

    per_tile = LANES // ROWS
    spread = force
    for turn in range(1, per_tile):
        spread = jnp.where(
            lax.rem(close, per_tile) == turn, pltpu.roll(force, turn * ROWS, 1), spread
        )
    tiles[close] = spread

    def f_copy(step, origin):
        return pltpu.make_async_remote_copy(
            src_ref=tiles.at[origin],
            dst_ref=tiles.at[origin],
            send_sem=f_send.at[step],
            recv_sem=f_recv.at[step],
            device_id={"group": far * n_near + near_peer(step)},
            device_id_type=MESH,
        )

    def g_copy(step, origin):
        return pltpu.make_async_remote_copy(
            src_ref=strip.at[origin],
            dst_ref=strip.at[origin],
            send_sem=g_send.at[step],
            recv_sem=g_recv.at[step],
            device_id={"group": far_peer(step) * n_near + close},
            device_id_type=MESH,
        )

    for step in range(1, n_near):
        f_copy(step, close).start()
    for step in range(1, n_near):
        f_copy(step, lax.rem(close + n_near - step, n_near)).wait_recv()
    n_strip = n_near // per_tile
    for t in range(n_strip):
        joined = tiles[per_tile * t]
        for i in range(1, per_tile):
            joined = joined + tiles[per_tile * t + i]
        strip[far, t] = joined
    for step in range(1, n_far):
        g_copy(step, far).start()
    for step in range(1, n_far):
        g_copy(step, lax.rem(far + n_far - step, n_far)).wait_recv()

    whole = my_start.astype(jnp.int32)
    tile_no, shift = whole // LANES, lax.rem(whole, LANES)
    left = jnp.zeros((8, LANES), jnp.float32)
    right = jnp.zeros((8, LANES), jnp.float32)
    for t in range(n_far * n_strip):
        value = strip[t // n_strip, t % n_strip]
        left = jnp.where(tile_no == t, value, left)
        if t > 0:
            right = jnp.where(tile_no == t - 1, value, right)
    window = jnp.concatenate([left, right], axis=1)
    bit = LANES // 2
    while bit:
        moved = pltpu.roll(window, 2 * LANES - bit, 1)
        window = jnp.where(lax.rem(shift // bit, 2) == 1, moved, window)
        bit //= 2
    out_ref[...] = jnp.where(lane < count, window[0:6, 0:LANES], 0.0)

    for step in range(1, n_far):
        a_copy(step, far).wait_send()
        g_copy(step, far).wait_send()
    for step in range(1, n_near):
        b_copy(step, close).wait_send()
        f_copy(step, close).wait_send()

    def drain(index, carry):
        peer = blk_peer(index)
        r_copy(peer, b).wait_send()
        p_copy(peer, b).wait_send()
        return carry

    lax.fori_loop(1, n_blk, drain, 0)


def on_device(
    low,
    n_near,
    star_pos,
    star_vel,
    star_acc,
    star_jerk,
    star_mass,
    star_dt,
    active_list,
    active_count,
):
    n_blk, n_group = lax.axis_size("blk"), lax.axis_size("group")
    n_far = n_group // n_near
    stars = star_mass.shape[0]
    slots = active_list.shape[2]
    dims = (n_blk, low, n_far, n_near, stars * n_blk)
    vmem = pl.BlockSpec(memory_space=pltpu.VMEM)
    f32, i32 = jnp.float32, jnp.int32
    dma = pltpu.SemaphoreType.DMA
    out = pl.pallas_call(
        functools.partial(kernel, dims),
        out_shape=jax.ShapeDtypeStruct((6, slots), f32),
        in_specs=[vmem] * 7 + [pl.BlockSpec(memory_space=pltpu.SMEM)],
        out_specs=vmem,
        scratch_shapes=[
            pltpu.VMEM((8, stars), f32),
            pltpu.VMEM((7, 8, stars), f32),
            pltpu.VMEM((n_far, 1, LANES), i32),
            pltpu.VMEM((n_near, n_far, 1, LANES), i32),
            pltpu.VMEM((n_blk, 8, LANES), f32),
            pltpu.VMEM((n_blk, 8, LANES), f32),
            pltpu.VMEM((n_blk, 8, LANES), f32),
            pltpu.VMEM((n_near, 8, LANES), f32),
            pltpu.VMEM((n_far, n_near * ROWS // LANES, 8, LANES), f32),
            dma((n_far,)),
            dma((n_far,)),
            dma((n_near,)),
            dma((n_near,)),
            dma((n_blk,)),
            dma((n_blk,)),
            dma((n_blk,)),
            dma((n_blk,)),
            dma((n_near,)),
            dma((n_near,)),
            dma((n_far,)),
            dma((n_far,)),
        ],
        compiler_params=pltpu.CompilerParams(collective_id=0, has_side_effects=True),
    )(
        star_pos,
        star_vel,
        star_acc,
        star_jerk,
        star_mass.reshape(1, stars),
        star_dt.reshape(1, stars),
        active_list.reshape(1, slots),
        active_count,
    )
    return out[None, None]


def solution(mesh):
    n_blk, n_group = mesh.shape["blk"], mesh.shape["group"]
    low = 8 if n_blk % 8 == 0 else n_blk
    n_near = 8 if n_group % 8 == 0 and n_group > 8 else 4
    return jax.shard_map(
        functools.partial(on_device, low, n_near),
        mesh=mesh,
        in_specs=(
            P(None, "blk"),
            P(None, "blk"),
            P(None, "blk"),
            P(None, "blk"),
            P("blk"),
            P("blk"),
            P("blk", "group", None),
            P("blk", "group"),
        ),
        out_specs=P("blk", "group", None, None),
        check_vma=False,
    )
```

```python
import functools

import jax
import jax.numpy as jnp
from jax import lax
from jax.experimental import pallas as pl
from jax.experimental.pallas import tpu as pltpu
from jax.sharding import PartitionSpec as P

MESH = pl.DeviceIdType.MESH
soften = 0.01
ROWS = 32
LANES = 128


def split(value):
    high = value.astype(jnp.bfloat16).astype(jnp.float32)
    rest = value - high
    middle = rest.astype(jnp.bfloat16).astype(jnp.float32)
    return high, middle, (rest - middle).astype(jnp.bfloat16).astype(jnp.float32)


def dot(left, right, transposed=False):
    dims = (((1,), (1 if transposed else 0,)), ((), ()))
    return lax.dot_general(left, right, dims, preferred_element_type=jnp.float32)


def kernel(
    dims,
    pos_ref,
    vel_ref,
    acc_ref,
    jerk_ref,
    mass_ref,
    dt_ref,
    list_ref,
    count_ref,
    out_ref,
    pos_in,
    vel_in,
    acc_in,
    jerk_in,
    mass_in,
    dt_in,
    list_in,
    exact,
    feature,
    cross,
    wide,
    near,
    lists,
    rows,
    res,
    part,
    tiles,
    strip,
    a_send,
    a_recv,
    b_send,
    b_recv,
    r_send,
    r_recv,
    p_send,
    p_recv,
    f_send,
    f_recv,
    g_send,
    g_recv,
    in_sem,
):
    n_blk, low, n_far, n_near, total_stars = dims
    high = n_blk // low
    stars = mass_ref.shape[1]
    n_group = n_far * n_near
    b = lax.axis_index("blk")
    g = lax.axis_index("group")
    far = g // n_near
    close = lax.rem(g, n_near)

    def far_peer(step):
        return lax.rem(far + step, n_far)

    def near_peer(step):
        return lax.rem(close + step, n_near)

    def blk_peer(place):
        if isinstance(place, int):
            rank = place
            if place >= 3:
                rank = low + 2 - place if place < 3 + low else n_blk + 2 - place
            turn = (rank + 1) // 2 if rank % 2 else (low - rank // 2) % low
            rise = 1 if high > 1 and 3 <= place < 3 + low else 0
        else:
            rank = jnp.where(place < 3 + low, low + 2 - place, n_blk + 2 - place)
            rank = jnp.where(place < 3, place, rank)
            turn = jnp.where(lax.rem(rank, 2) == 1, (rank + 1) // 2, lax.rem(low - rank // 2, low))
            rise = jnp.int32(0)
            if high > 1:
                rise = jnp.where((place >= 3) & (place < 3 + low), 1, 0)
        row = lax.rem(b // low + rise, high)
        return row * low + lax.rem(lax.rem(b, low) + turn, low)

    fetch = [
        pltpu.make_async_copy(source, target, in_sem.at[place])
        for place, (source, target) in enumerate(
            [
                (pos_ref, pos_in),
                (vel_ref, vel_in),
                (acc_ref, acc_in),
                (jerk_ref, jerk_in),
                (mass_ref, mass_in),
                (dt_ref, dt_in),
                (list_ref, list_in),
            ]
        )
    ]
    for copy in fetch:
        copy.start()

    barrier = pltpu.get_barrier_semaphore()
    for step in range(1, n_far):
        pl.semaphore_signal(
            barrier, 1, device_id={"group": far_peer(step) * n_near + close}, device_id_type=MESH
        )
    for step in range(1, n_near):
        pl.semaphore_signal(
            barrier, 1, device_id={"group": far * n_near + near_peer(step)}, device_id_type=MESH
        )
    for step in range(1, n_blk):
        pl.semaphore_signal(
            barrier, 1, device_id={"blk": lax.rem(b + step, n_blk)}, device_id_type=MESH
        )

    for copy in fetch:
        copy.wait()
    count = count_ref[0, 0]
    lane = lax.broadcasted_iota(jnp.int32, (1, LANES), 1)
    near[far] = jnp.where(lane < count, list_in[...], -1)

    width = min(1024, stars)

    def predict(index, carry):
        here = pl.ds(pl.multiple_of(index * width, width), width)
        step = dt_in[:, here]
        vel, acc, jerk = vel_in[:, here], acc_in[:, here], jerk_in[:, here]
        ppos = pos_in[:, here] + step * (vel + step * (0.5 * acc + step * (jerk / 6.0)))
        pvel = vel + step * (acc + step * (0.5 * jerk))
        weight = mass_in[:, here] / total_stars
        blank = jnp.zeros_like(weight)
        for row in range(3):
            wide[row, :, here] = jnp.broadcast_to(ppos[row : row + 1], (8, width))
        state = jnp.concatenate([ppos, pvel, blank, blank], axis=0)
        eight = jnp.zeros_like(state)
        exact[:, here] = jnp.concatenate([*split(state), eight], axis=0).astype(jnp.bfloat16)
        scaled = jnp.concatenate([ppos * weight, pvel * weight, weight, blank], axis=0)
        feature[:, here] = jnp.concatenate([*split(scaled), eight], axis=0).astype(jnp.bfloat16)
        inner = jnp.sum(ppos * pvel, axis=0, keepdims=True)
        mixed = jnp.concatenate([ppos, pvel, inner, blank + 1.0], axis=0) * weight
        big, mid, small = split(mixed)
        cross[:, here] = jnp.concatenate([big, mid, big, mid, small, big], axis=0).astype(
            jnp.bfloat16
        )
        return carry

    lax.fori_loop(0, stars // width, predict, 0)

    pl.semaphore_wait(barrier, (n_far - 1) + (n_near - 1) + (n_blk - 1))

    def a_copy(step, origin):
        return pltpu.make_async_remote_copy(
            src_ref=near.at[origin],
            dst_ref=near.at[origin],
            send_sem=a_send.at[step],
            recv_sem=a_recv.at[step],
            device_id={"group": far_peer(step) * n_near + close},
            device_id_type=MESH,
        )

    def b_copy(step, origin):
        return pltpu.make_async_remote_copy(
            src_ref=near,
            dst_ref=lists.at[origin],
            send_sem=b_send.at[step],
            recv_sem=b_recv.at[step],
            device_id={"group": far * n_near + near_peer(step)},
            device_id_type=MESH,
        )

    for step in range(1, n_far):
        a_copy(step, far).start()
    for step in range(1, n_far):
        a_copy(step, lax.rem(far + n_far - step, n_far)).wait_recv()
    for step in range(1, n_near):
        b_copy(step, close).start()
    lists[close] = near[...]
    for step in range(1, n_near):
        b_copy(step, lax.rem(close + n_near - step, n_near)).wait_recv()

    entry = lists[...].reshape(n_group, LANES)
    valid = entry >= 0
    validf = jnp.where(valid, 1.0, 0.0).astype(jnp.float32)
    entryf = entry.astype(jnp.float32)
    r_iota = lax.broadcasted_iota(jnp.int32, (n_group, n_group), 0)
    c_iota = lax.broadcasted_iota(jnp.int32, (n_group, n_group), 1)
    before = jnp.where(c_iota < r_iota, 1.0, 0.0).astype(jnp.float32)
    starts = jnp.sum(
        jnp.dot(before, validf, preferred_element_type=jnp.float32), axis=1, keepdims=True
    )
    slot = lax.broadcasted_iota(jnp.int32, (n_group, LANES), 1).astype(jnp.float32)
    base = (g * ROWS).astype(jnp.float32)
    place = jnp.where(valid, starts + slot - base, -1.0)
    mine = close * n_far + far
    owner_row = lax.broadcasted_iota(jnp.int32, (n_group, LANES), 0)
    my_start = jnp.sum(
        jnp.sum(jnp.where(owner_row < mine, validf, 0.0), axis=1, keepdims=True),
        axis=0,
        keepdims=True,
    )
    found = jnp.concatenate(
        [
            jnp.sum(jnp.where(place == float(s), entryf, 0.0), axis=0, keepdims=True)
            for s in range(ROWS)
        ],
        axis=0,
    )
    chosen = jnp.sum(found, axis=1, keepdims=True).astype(jnp.int32)
    column = lax.broadcasted_iota(jnp.int32, (ROWS, width), 1)

    def gather(index, total):
        here = pl.ds(pl.multiple_of(index * width, width), width)
        hot = jnp.where(column + index * width == chosen, 1.0, 0.0).astype(jnp.bfloat16)
        return total + dot(exact[:, here], hot, True)

    picked = lax.fori_loop(
        0, stars // width, gather, jnp.zeros((32, ROWS), jnp.float32), unroll=True
    )
    picked = (picked[0:8] + picked[8:16]) + picked[16:24]
    rows[b] = jnp.concatenate([picked, jnp.zeros((8, LANES - ROWS), jnp.float32)], axis=1)

    def r_copy(peer, origin):
        return pltpu.make_async_remote_copy(
            src_ref=rows.at[origin],
            dst_ref=rows.at[origin],
            send_sem=r_send.at[peer],
            recv_sem=r_recv.at[origin],
            device_id={"blk": peer},
            device_id_type=MESH,
        )

    def p_copy(peer, origin):
        return pltpu.make_async_remote_copy(
            src_ref=res.at[peer],
            dst_ref=part.at[origin],
            send_sem=p_send.at[peer],
            recv_sem=p_recv.at[origin],
            device_id={"blk": peer},
            device_id_type=MESH,
        )

    for index in range(1, n_blk):
        r_copy(blk_peer(index), b).start()

    span = min(2048, stars)
    out_lane = lax.broadcasted_iota(jnp.int32, (ROWS, LANES), 1)

    def pairs(index, carry):
        peer = blk_peer(index)

        @pl.when(index > 0)
        def _():
            r_copy(peer, peer).wait_recv()

        own = rows[peer]
        own_pos, own_vel = own[0:3], own[3:6]
        inner = jnp.sum(own_pos * own_vel, axis=0, keepdims=True)
        mixed = jnp.concatenate([-own_vel, -own_pos, jnp.ones_like(inner), inner], axis=0)
        big, mid, small = split(mixed)
        fill = jnp.zeros((LANES - 56, LANES), jnp.float32)
        down = jnp.transpose(
            jnp.concatenate([big, big, mid, mid, big, small, own, fill], axis=0)
        )
        mine_mixed = down[0:ROWS, 0:48].astype(jnp.bfloat16)
        across = [jnp.broadcast_to(down[0:ROWS, 48 + c : 49 + c], (ROWS, LANES)) for c in range(3)]

        def advance(tile, carried):
            sums, sx, sy, sz = carried
            base = pl.multiple_of(tile * span, span)
            here = pl.ds(base, span)
            turning = dot(mine_mixed, cross[:, here])
            tops, rests = [], []
            for part_at in range(0, span, LANES):
                at = pl.ds(pl.multiple_of(base + part_at, LANES), LANES)
                rx, ry, rz = (
                    jnp.concatenate([wide[c, :, at]] * (ROWS // 8), axis=0) - across[c]
                    for c in range(3)
                )
                inverse = lax.rsqrt((rx * rx + ry * ry) + (rz * rz + soften))
                square = inverse * inverse
                cube = inverse * square
                swing = (turning[:, part_at : part_at + LANES] * square) * cube
                sx, sy, sz = sx + swing * rx, sy + swing * ry, sz + swing * rz
                top = cube.astype(jnp.bfloat16)
                tops.append(top)
                rests.append((cube - top.astype(jnp.float32)).astype(jnp.bfloat16))
            product = dot(jnp.concatenate(tops, axis=1), feature[:, here], True) + dot(
                jnp.concatenate(rests, axis=1), feature[:, here], True
            )
            return sums + product, sx, sy, sz

        zero = jnp.zeros((ROWS, LANES), jnp.float32)
        sums, sx, sy, sz = lax.fori_loop(
            0,
            stars // span,
            advance,
            (jnp.zeros((ROWS, 32), jnp.float32), zero, zero, zero),
            unroll=True,
        )
        piece = jnp.concatenate([sums, jnp.zeros((ROWS, LANES - 32), jnp.float32)], axis=1)
        for c, total in enumerate((sx, sy, sz)):
            piece = jnp.where(out_lane == 32 + c, jnp.sum(total, axis=1, keepdims=True), piece)
        up = jnp.transpose(
            jnp.concatenate([piece, jnp.zeros((LANES - ROWS, LANES), jnp.float32)], axis=0)
        )
        moment = (up[0:8] + up[8:16]) + up[16:24]
        weighed = moment[6:7]
        accel = moment[0:3] - own_pos * weighed
        jerks = (moment[3:6] - own_vel * weighed) - 3.0 * up[32:35]
        result = jnp.concatenate([accel, jerks, jnp.zeros((2, LANES), jnp.float32)], axis=0)

        @pl.when(index == 0)
        def _():
            part[b] = result

        @pl.when(index > 0)
        def _():
            res[peer] = result
            p_copy(peer, b).start()

        return carry

    lax.fori_loop(0, n_blk, pairs, 0)

    for index in range(1, n_blk):
        peer = blk_peer(index)
        p_copy(peer, peer).wait_recv()
    force = jnp.sum(part[...], axis=0)

    per_tile = LANES // ROWS
    spread = force
    for turn in range(1, per_tile):
        spread = jnp.where(
            lax.rem(close, per_tile) == turn, pltpu.roll(force, turn * ROWS, 1), spread
        )
    tiles[close] = spread

    def f_copy(step, origin):
        return pltpu.make_async_remote_copy(
            src_ref=tiles.at[origin],
            dst_ref=tiles.at[origin],
            send_sem=f_send.at[step],
            recv_sem=f_recv.at[step],
            device_id={"group": far * n_near + near_peer(step)},
            device_id_type=MESH,
        )

    def g_copy(step, origin):
        return pltpu.make_async_remote_copy(
            src_ref=strip.at[origin],
            dst_ref=strip.at[origin],
            send_sem=g_send.at[step],
            recv_sem=g_recv.at[step],
            device_id={"group": far_peer(step) * n_near + close},
            device_id_type=MESH,
        )

    for step in range(1, n_near):
        f_copy(step, close).start()
    for step in range(1, n_near):
        f_copy(step, lax.rem(close + n_near - step, n_near)).wait_recv()
    n_strip = n_near // per_tile
    for t in range(n_strip):
        joined = tiles[per_tile * t]
        for i in range(1, per_tile):
            joined = joined + tiles[per_tile * t + i]
        strip[far, t] = joined
    for step in range(1, n_far):
        g_copy(step, far).start()
    for step in range(1, n_far):
        g_copy(step, lax.rem(far + n_far - step, n_far)).wait_recv()

    whole = my_start.astype(jnp.int32)
    tile_no, shift = whole // LANES, lax.rem(whole, LANES)
    left = jnp.zeros((8, LANES), jnp.float32)
    right = jnp.zeros((8, LANES), jnp.float32)
    for t in range(n_far * n_strip):
        value = strip[t // n_strip, t % n_strip]
        left = jnp.where(tile_no == t, value, left)
        if t > 0:
            right = jnp.where(tile_no == t - 1, value, right)
    window = jnp.concatenate([left, right], axis=1)
    bit = LANES // 2
    while bit:
        moved = pltpu.roll(window, 2 * LANES - bit, 1)
        window = jnp.where(lax.rem(shift // bit, 2) == 1, moved, window)
        bit //= 2
    out_ref[:, 0, :] = jnp.where(lane < count, window[0:6, 0:LANES], 0.0)

    for step in range(1, n_far):
        a_copy(step, far).wait_send()
        g_copy(step, far).wait_send()
    for step in range(1, n_near):
        b_copy(step, close).wait_send()
        f_copy(step, close).wait_send()

    for index in range(1, n_blk):
        peer = blk_peer(index)
        r_copy(peer, b).wait_send()
        p_copy(peer, b).wait_send()


def on_device(
    low,
    n_near,
    star_pos,
    star_vel,
    star_acc,
    star_jerk,
    star_mass,
    star_dt,
    active_list,
    active_count,
):
    n_blk, n_group = lax.axis_size("blk"), lax.axis_size("group")
    n_far = n_group // n_near
    stars = star_mass.shape[0]
    slots = active_list.shape[2]
    dims = (n_blk, low, n_far, n_near, stars * n_blk)
    vmem = pl.BlockSpec(memory_space=pltpu.VMEM)
    f32, i32, bf16 = jnp.float32, jnp.int32, jnp.bfloat16
    dma = pltpu.SemaphoreType.DMA
    out = pl.pallas_call(
        functools.partial(kernel, dims),
        out_shape=jax.ShapeDtypeStruct((6, 1, slots), f32),
        in_specs=[pl.BlockSpec(memory_space=pl.ANY)] * 7 + [pl.BlockSpec(memory_space=pltpu.SMEM)],
        out_specs=vmem,
        scratch_shapes=[
            *[pltpu.VMEM((3, stars), f32)] * 4,
            pltpu.VMEM((1, stars), f32),
            pltpu.VMEM((1, stars), f32),
            pltpu.VMEM((1, slots), i32),
            pltpu.VMEM((32, stars), bf16),
            pltpu.VMEM((32, stars), bf16),
            pltpu.VMEM((48, stars), bf16),
            pltpu.VMEM((3, 8, stars), f32),
            pltpu.VMEM((n_far, 1, LANES), i32),
            pltpu.VMEM((n_near, n_far, 1, LANES), i32),
            pltpu.VMEM((n_blk, 8, LANES), f32),
            pltpu.VMEM((n_blk, 8, LANES), f32),
            pltpu.VMEM((n_blk, 8, LANES), f32),
            pltpu.VMEM((n_near, 8, LANES), f32),
            pltpu.VMEM((n_far, n_near * ROWS // LANES, 8, LANES), f32),
            dma((n_far,)),
            dma((n_far,)),
            dma((n_near,)),
            dma((n_near,)),
            dma((n_blk,)),
            dma((n_blk,)),
            dma((n_blk,)),
            dma((n_blk,)),
            dma((n_near,)),
            dma((n_near,)),
            dma((n_far,)),
            dma((n_far,)),
            dma((7,)),
        ],
        compiler_params=pltpu.CompilerParams(collective_id=0, has_side_effects=True),
    )(
        star_pos,
        star_vel,
        star_acc,
        star_jerk,
        star_mass.reshape(1, stars),
        star_dt.reshape(1, stars),
        active_list.reshape(1, slots),
        active_count,
    )
    return out.reshape(1, 1, 6, slots)


def solution(mesh):
    n_blk, n_group = mesh.shape["blk"], mesh.shape["group"]
    low = 8 if n_blk % 8 == 0 else n_blk
    n_near = 8 if n_group % 8 == 0 and n_group > 8 else 4
    return jax.shard_map(
        functools.partial(on_device, low, n_near),
        mesh=mesh,
        in_specs=(
            P(None, "blk"),
            P(None, "blk"),
            P(None, "blk"),
            P(None, "blk"),
            P("blk"),
            P("blk"),
            P("blk", "group", None),
            P("blk", "group"),
        ),
        out_specs=P("blk", "group", None, None),
        check_vma=False,
    )
```

```python
import functools

import jax
import jax.numpy as jnp
from jax import lax
from jax.experimental import pallas as pl
from jax.experimental.pallas import tpu as pltpu
from jax.sharding import PartitionSpec as P

MESH = pl.DeviceIdType.MESH
soften = 0.01
ROWS = 32
LANES = 128


def split(value):
    high = value.astype(jnp.bfloat16).astype(jnp.float32)
    rest = value - high
    middle = rest.astype(jnp.bfloat16).astype(jnp.float32)
    return high, middle, (rest - middle).astype(jnp.bfloat16).astype(jnp.float32)


def dot(left, right, transposed=False):
    dims = (((1,), (1 if transposed else 0,)), ((), ()))
    return lax.dot_general(left, right, dims, preferred_element_type=jnp.float32)


def kernel(
    dims,
    pos_ref,
    vel_ref,
    acc_ref,
    jerk_ref,
    mass_ref,
    dt_ref,
    list_ref,
    count_ref,
    out_ref,
    pos_in,
    vel_in,
    acc_in,
    jerk_in,
    mass_in,
    dt_in,
    list_in,
    exact,
    feature,
    cross,
    wide,
    near,
    lists,
    rows,
    res,
    part,
    tiles,
    strip,
    a_send,
    a_recv,
    b_send,
    b_recv,
    r_send,
    r_recv,
    p_send,
    p_recv,
    f_send,
    f_recv,
    g_send,
    g_recv,
    in_sem,
):
    n_blk, low, n_far, n_near, total_stars = dims
    high = n_blk // low
    stars = mass_ref.shape[1]
    n_group = n_far * n_near
    b = lax.axis_index("blk")
    g = lax.axis_index("group")
    far = g // n_near
    close = lax.rem(g, n_near)

    def far_peer(step):
        return lax.rem(far + step, n_far)

    def near_peer(step):
        return lax.rem(close + step, n_near)

    early = max(1, low // 2)
    row, column = b // low, lax.rem(b, low)
    other = lax.rem(row + 1, high)

    def peer_at(place):
        if isinstance(place, int):
            spot = place if place < early else place - (early if place < early + low else low)
            rank = spot if spot < 3 else low + 2 - spot
            turn = (rank + 1) // 2 if rank % 2 else (low - rank // 2) % low
            return lax.rem(column + turn, low)
        spot = jnp.where(place < early + low, place - early, place - low)
        spot = jnp.where(place < early, place, spot)
        rank = jnp.where(spot < 3, spot, low + 2 - spot)
        turn = jnp.where(lax.rem(rank, 2) == 1, (rank + 1) // 2, lax.rem(low - rank // 2, low))
        return lax.rem(column + turn, low)

    fetch = [
        pltpu.make_async_copy(source, target, in_sem.at[place])
        for place, (source, target) in enumerate(
            [
                (pos_ref, pos_in),
                (vel_ref, vel_in),
                (acc_ref, acc_in),
                (jerk_ref, jerk_in),
                (mass_ref, mass_in),
                (dt_ref, dt_in),
                (list_ref, list_in),
            ]
        )
    ]
    for copy in fetch:
        copy.start()

    barrier = pltpu.get_barrier_semaphore()
    for step in range(1, n_far):
        pl.semaphore_signal(
            barrier, 1, device_id={"group": far_peer(step) * n_near + close}, device_id_type=MESH
        )
    for step in range(1, n_near):
        pl.semaphore_signal(
            barrier, 1, device_id={"group": far * n_near + near_peer(step)}, device_id_type=MESH
        )
    for step in range(1, low):
        side = row * low + lax.rem(column + step, low)
        pl.semaphore_signal(barrier, 1, device_id={"blk": side}, device_id_type=MESH)
    pl.semaphore_signal(barrier, 1, device_id={"blk": other * low + column}, device_id_type=MESH)

    for copy in fetch:
        copy.wait()
    count = count_ref[0, 0]
    lane = lax.broadcasted_iota(jnp.int32, (1, LANES), 1)
    near[far] = jnp.where(lane < count, list_in[...], -1)

    width = min(1024, stars)

    def predict(index, carry):
        here = pl.ds(pl.multiple_of(index * width, width), width)
        step = dt_in[:, here]
        vel, acc, jerk = vel_in[:, here], acc_in[:, here], jerk_in[:, here]
        ppos = pos_in[:, here] + step * (vel + step * (0.5 * acc + step * (jerk / 6.0)))
        pvel = vel + step * (acc + step * (0.5 * jerk))
        weight = mass_in[:, here] / total_stars
        blank = jnp.zeros_like(weight)
        for row in range(3):
            wide[row, :, here] = jnp.broadcast_to(ppos[row : row + 1], (8, width))
        state = jnp.concatenate([ppos, pvel, blank, blank], axis=0)
        eight = jnp.zeros_like(state)
        exact[:, here] = jnp.concatenate([*split(state), eight], axis=0).astype(jnp.bfloat16)
        scaled = jnp.concatenate([ppos * weight, pvel * weight, weight, blank], axis=0)
        feature[:, here] = jnp.concatenate([*split(scaled), eight], axis=0).astype(jnp.bfloat16)
        inner = jnp.sum(ppos * pvel, axis=0, keepdims=True)
        mixed = jnp.concatenate([ppos, pvel, inner, blank + 1.0], axis=0) * weight
        big, mid, small = split(mixed)
        cross[:, here] = jnp.concatenate([big, mid, big, mid, small, big], axis=0).astype(
            jnp.bfloat16
        )
        return carry

    lax.fori_loop(0, stars // width, predict, 0)

    pl.semaphore_wait(barrier, (n_far - 1) + (n_near - 1) + low)

    def a_copy(step, origin):
        return pltpu.make_async_remote_copy(
            src_ref=near.at[origin],
            dst_ref=near.at[origin],
            send_sem=a_send.at[step],
            recv_sem=a_recv.at[step],
            device_id={"group": far_peer(step) * n_near + close},
            device_id_type=MESH,
        )

    def b_copy(step, origin):
        return pltpu.make_async_remote_copy(
            src_ref=near,
            dst_ref=lists.at[origin],
            send_sem=b_send.at[step],
            recv_sem=b_recv.at[step],
            device_id={"group": far * n_near + near_peer(step)},
            device_id_type=MESH,
        )

    for step in range(1, n_far):
        a_copy(step, far).start()
    for step in range(1, n_far):
        a_copy(step, lax.rem(far + n_far - step, n_far)).wait_recv()
    for step in range(1, n_near):
        b_copy(step, close).start()
    lists[close] = near[...]
    for step in range(1, n_near):
        b_copy(step, lax.rem(close + n_near - step, n_near)).wait_recv()

    entry = lists[...].reshape(n_group, LANES)
    valid = entry >= 0
    validf = jnp.where(valid, 1.0, 0.0).astype(jnp.float32)
    entryf = entry.astype(jnp.float32)
    r_iota = lax.broadcasted_iota(jnp.int32, (n_group, n_group), 0)
    c_iota = lax.broadcasted_iota(jnp.int32, (n_group, n_group), 1)
    before = jnp.where(c_iota < r_iota, 1.0, 0.0).astype(jnp.float32)
    starts = jnp.sum(
        jnp.dot(before, validf, preferred_element_type=jnp.float32), axis=1, keepdims=True
    )
    slot = lax.broadcasted_iota(jnp.int32, (n_group, LANES), 1).astype(jnp.float32)
    base = (g * ROWS).astype(jnp.float32)
    place = jnp.where(valid, starts + slot - base, -1.0)
    mine = close * n_far + far
    owner_row = lax.broadcasted_iota(jnp.int32, (n_group, LANES), 0)
    my_start = jnp.sum(
        jnp.sum(jnp.where(owner_row < mine, validf, 0.0), axis=1, keepdims=True),
        axis=0,
        keepdims=True,
    )
    found = jnp.concatenate(
        [
            jnp.sum(jnp.where(place == float(s), entryf, 0.0), axis=0, keepdims=True)
            for s in range(ROWS)
        ],
        axis=0,
    )
    chosen = jnp.sum(found, axis=1, keepdims=True).astype(jnp.int32)
    star_no = lax.broadcasted_iota(jnp.int32, (ROWS, width), 1)

    def gather(index, total):
        here = pl.ds(pl.multiple_of(index * width, width), width)
        hot = jnp.where(star_no + index * width == chosen, 1.0, 0.0).astype(jnp.bfloat16)
        return total + dot(exact[:, here], hot, True)

    picked = lax.fori_loop(
        0, stars // width, gather, jnp.zeros((32, ROWS), jnp.float32), unroll=True
    )
    picked = (picked[0:8] + picked[8:16]) + picked[16:24]
    rows[b] = jnp.concatenate([picked, jnp.zeros((8, LANES - ROWS), jnp.float32)], axis=1)

    def r_copy(peer, origin, mark):
        return pltpu.make_async_remote_copy(
            src_ref=rows.at[origin],
            dst_ref=rows.at[origin],
            send_sem=r_send.at[mark],
            recv_sem=r_recv.at[origin],
            device_id={"blk": peer},
            device_id_type=MESH,
        )

    def p_copy(peer, source, slot):
        return pltpu.make_async_remote_copy(
            src_ref=res.at[source],
            dst_ref=part.at[slot],
            send_sem=p_send.at[source],
            recv_sem=p_recv.at[slot],
            device_id={"blk": peer},
            device_id_type=MESH,
        )

    partner = other * low + column
    sum_copy = pltpu.make_async_remote_copy(
        src_ref=res.at[partner],
        dst_ref=part.at[n_blk],
        send_sem=p_send.at[partner],
        recv_sem=p_recv.at[n_blk],
        device_id={"blk": partner},
        device_id_type=MESH,
    )

    def side(step):
        return lax.rem(column + step, low)

    r_copy(partner, b, partner).start()
    for place in list(range(1, early)) + list(range(early + low, n_blk)):
        peer = row * low + peer_at(place)
        r_copy(peer, b, peer).start()

    span = min(2048, stars)
    out_lane = lax.broadcasted_iota(jnp.int32, (ROWS, LANES), 1)

    def pairs(index, carry):
        line = peer_at(index)
        away = (index >= early) & (index < early + low)
        peer = jnp.where(away, other, row) * low + line

        @pl.when(index == min(3, early))
        def _():
            r_copy(partner, partner, partner).wait_recv()
            for step in range(1, low):
                r_copy(row * low + side(step), partner, other * low + side(step)).start()

        @pl.when((index > 0) & (index != early))
        def _():
            r_copy(peer, peer, peer).wait_recv()

        @pl.when(index == n_blk - 1)
        def _():
            for step in range(1, low):
                slot = other * low + side(low - step)
                p_copy(b, slot, slot).wait_recv()
            res[partner] = jnp.sum(part[pl.ds(other * low, low)], axis=0)
            sum_copy.start()

        own = rows[peer]
        own_pos, own_vel = own[0:3], own[3:6]
        inner = jnp.sum(own_pos * own_vel, axis=0, keepdims=True)
        mixed = jnp.concatenate([-own_vel, -own_pos, jnp.ones_like(inner), inner], axis=0)
        big, mid, small = split(mixed)
        fill = jnp.zeros((LANES - 56, LANES), jnp.float32)
        down = jnp.transpose(
            jnp.concatenate([big, big, mid, mid, big, small, own, fill], axis=0)
        )
        mine_mixed = down[0:ROWS, 0:48].astype(jnp.bfloat16)
        across = [jnp.broadcast_to(down[0:ROWS, 48 + c : 49 + c], (ROWS, LANES)) for c in range(3)]

        def advance(tile, carried):
            sums, sx, sy, sz = carried
            base = pl.multiple_of(tile * span, span)
            here = pl.ds(base, span)
            turning = dot(mine_mixed, cross[:, here])
            tops, rests = [], []
            for part_at in range(0, span, LANES):
                at = pl.ds(pl.multiple_of(base + part_at, LANES), LANES)
                rx, ry, rz = (
                    jnp.concatenate([wide[c, :, at]] * (ROWS // 8), axis=0) - across[c]
                    for c in range(3)
                )
                inverse = lax.rsqrt((rx * rx + ry * ry) + (rz * rz + soften))
                square = inverse * inverse
                cube = inverse * square
                swing = (turning[:, part_at : part_at + LANES] * square) * cube
                sx, sy, sz = sx + swing * rx, sy + swing * ry, sz + swing * rz
                top = cube.astype(jnp.bfloat16)
                tops.append(top)
                rests.append((cube - top.astype(jnp.float32)).astype(jnp.bfloat16))
            product = dot(jnp.concatenate(tops, axis=1), feature[:, here], True) + dot(
                jnp.concatenate(rests, axis=1), feature[:, here], True
            )
            return sums + product, sx, sy, sz

        zero = jnp.zeros((ROWS, LANES), jnp.float32)
        sums, sx, sy, sz = lax.fori_loop(
            0,
            stars // span,
            advance,
            (jnp.zeros((ROWS, 32), jnp.float32), zero, zero, zero),
            unroll=True,
        )
        piece = jnp.concatenate([sums, jnp.zeros((ROWS, LANES - 32), jnp.float32)], axis=1)
        for c, total in enumerate((sx, sy, sz)):
            piece = jnp.where(out_lane == 32 + c, jnp.sum(total, axis=1, keepdims=True), piece)
        up = jnp.transpose(
            jnp.concatenate([piece, jnp.zeros((LANES - ROWS, LANES), jnp.float32)], axis=0)
        )
        moment = (up[0:8] + up[8:16]) + up[16:24]
        weighed = moment[6:7]
        accel = moment[0:3] - own_pos * weighed
        jerks = (moment[3:6] - own_vel * weighed) - 3.0 * up[32:35]
        result = jnp.concatenate([accel, jerks, jnp.zeros((2, LANES), jnp.float32)], axis=0)

        @pl.when(index == 0)
        def _():
            part[b] = result

        @pl.when(index == early)
        def _():
            part[partner] = result

        @pl.when((index > 0) & (index != early))
        def _():
            res[peer] = result
            p_copy(row * low + line, peer, jnp.where(away, other, row) * low + column).start()

        return carry

    lax.fori_loop(0, n_blk, pairs, 0)

    for step in range(1, low):
        slot = row * low + side(low - step)
        p_copy(b, slot, slot).wait_recv()
    sum_copy.wait_recv()
    force = jnp.sum(part[pl.ds(row * low, low)], axis=0) + part[n_blk]

    per_tile = LANES // ROWS
    spread = force
    for turn in range(1, per_tile):
        spread = jnp.where(
            lax.rem(close, per_tile) == turn, pltpu.roll(force, turn * ROWS, 1), spread
        )
    tiles[close] = spread

    def f_copy(step, origin):
        return pltpu.make_async_remote_copy(
            src_ref=tiles.at[origin],
            dst_ref=tiles.at[origin],
            send_sem=f_send.at[step],
            recv_sem=f_recv.at[step],
            device_id={"group": far * n_near + near_peer(step)},
            device_id_type=MESH,
        )

    def g_copy(step, origin):
        return pltpu.make_async_remote_copy(
            src_ref=strip.at[origin],
            dst_ref=strip.at[origin],
            send_sem=g_send.at[step],
            recv_sem=g_recv.at[step],
            device_id={"group": far_peer(step) * n_near + close},
            device_id_type=MESH,
        )

    for step in range(1, n_near):
        f_copy(step, close).start()
    for step in range(1, n_near):
        f_copy(step, lax.rem(close + n_near - step, n_near)).wait_recv()
    n_strip = n_near // per_tile
    for t in range(n_strip):
        joined = tiles[per_tile * t]
        for i in range(1, per_tile):
            joined = joined + tiles[per_tile * t + i]
        strip[far, t] = joined
    for step in range(1, n_far):
        g_copy(step, far).start()
    for step in range(1, n_far):
        a_copy(step, far).wait_send()
    for step in range(1, n_near):
        b_copy(step, close).wait_send()
        f_copy(step, close).wait_send()
    r_copy(partner, b, partner).wait_send()
    sum_copy.wait_send()
    for step in range(1, low):
        near_mark, far_mark = row * low + side(step), other * low + side(step)
        r_copy(near_mark, b, near_mark).wait_send()
        r_copy(near_mark, partner, far_mark).wait_send()
        p_copy(near_mark, near_mark, b).wait_send()
        p_copy(near_mark, far_mark, partner).wait_send()
    for step in range(1, n_far):
        g_copy(step, lax.rem(far + n_far - step, n_far)).wait_recv()

    whole = my_start.astype(jnp.int32)
    tile_no, shift = whole // LANES, lax.rem(whole, LANES)
    left = jnp.zeros((8, LANES), jnp.float32)
    right = jnp.zeros((8, LANES), jnp.float32)
    for t in range(n_far * n_strip):
        value = strip[t // n_strip, t % n_strip]
        left = jnp.where(tile_no == t, value, left)
        if t > 0:
            right = jnp.where(tile_no == t - 1, value, right)
    window = jnp.concatenate([left, right], axis=1)
    bit = LANES // 2
    while bit:
        moved = pltpu.roll(window, 2 * LANES - bit, 1)
        window = jnp.where(lax.rem(shift // bit, 2) == 1, moved, window)
        bit //= 2
    out_ref[:, 0, :] = jnp.where(lane < count, window[0:6, 0:LANES], 0.0)

    for step in range(1, n_far):
        g_copy(step, far).wait_send()


def on_device(
    low,
    n_near,
    star_pos,
    star_vel,
    star_acc,
    star_jerk,
    star_mass,
    star_dt,
    active_list,
    active_count,
):
    n_blk, n_group = lax.axis_size("blk"), lax.axis_size("group")
    n_far = n_group // n_near
    stars = star_mass.shape[0]
    slots = active_list.shape[2]
    dims = (n_blk, low, n_far, n_near, stars * n_blk)
    vmem = pl.BlockSpec(memory_space=pltpu.VMEM)
    f32, i32, bf16 = jnp.float32, jnp.int32, jnp.bfloat16
    dma = pltpu.SemaphoreType.DMA
    out = pl.pallas_call(
        functools.partial(kernel, dims),
        out_shape=jax.ShapeDtypeStruct((6, 1, slots), f32),
        in_specs=[pl.BlockSpec(memory_space=pl.ANY)] * 7 + [pl.BlockSpec(memory_space=pltpu.SMEM)],
        out_specs=vmem,
        scratch_shapes=[
            *[pltpu.VMEM((3, stars), f32)] * 4,
            pltpu.VMEM((1, stars), f32),
            pltpu.VMEM((1, stars), f32),
            pltpu.VMEM((1, slots), i32),
            pltpu.VMEM((32, stars), bf16),
            pltpu.VMEM((32, stars), bf16),
            pltpu.VMEM((48, stars), bf16),
            pltpu.VMEM((3, 8, stars), f32),
            pltpu.VMEM((n_far, 1, LANES), i32),
            pltpu.VMEM((n_near, n_far, 1, LANES), i32),
            pltpu.VMEM((n_blk, 8, LANES), f32),
            pltpu.VMEM((n_blk, 8, LANES), f32),
            pltpu.VMEM((n_blk + 1, 8, LANES), f32),
            pltpu.VMEM((n_near, 8, LANES), f32),
            pltpu.VMEM((n_far, n_near * ROWS // LANES, 8, LANES), f32),
            dma((n_far,)),
            dma((n_far,)),
            dma((n_near,)),
            dma((n_near,)),
            dma((n_blk,)),
            dma((n_blk,)),
            dma((n_blk,)),
            dma((n_blk + 1,)),
            dma((n_near,)),
            dma((n_near,)),
            dma((n_far,)),
            dma((n_far,)),
            dma((7,)),
        ],
        compiler_params=pltpu.CompilerParams(collective_id=0, has_side_effects=True),
    )(
        star_pos,
        star_vel,
        star_acc,
        star_jerk,
        star_mass.reshape(1, stars),
        star_dt.reshape(1, stars),
        active_list.reshape(1, slots),
        active_count,
    )
    return out.reshape(1, 1, 6, slots)


def solution(mesh):
    n_blk, n_group = mesh.shape["blk"], mesh.shape["group"]
    low = n_blk // 2
    n_near = 8 if n_group % 8 == 0 and n_group > 8 else 4
    return jax.shard_map(
        functools.partial(on_device, low, n_near),
        mesh=mesh,
        in_specs=(
            P(None, "blk"),
            P(None, "blk"),
            P(None, "blk"),
            P(None, "blk"),
            P("blk"),
            P("blk"),
            P("blk", "group", None),
            P("blk", "group"),
        ),
        out_specs=P("blk", "group", None, None),
        check_vma=False,
    )
```

```python
import functools

import jax
import jax.numpy as jnp
from jax import lax
from jax.experimental import pallas as pl
from jax.experimental.pallas import tpu as pltpu
from jax.sharding import PartitionSpec as P

MESH = pl.DeviceIdType.MESH
soften = 0.01
ROWS = 32
LANES = 128


def split(value):
    high = value.astype(jnp.bfloat16).astype(jnp.float32)
    rest = value - high
    middle = rest.astype(jnp.bfloat16).astype(jnp.float32)
    return high, middle, (rest - middle).astype(jnp.bfloat16).astype(jnp.float32)


def dot(left, right, transposed=False):
    dims = (((1,), (1 if transposed else 0,)), ((), ()))
    return lax.dot_general(left, right, dims, preferred_element_type=jnp.float32)


def kernel(
    dims,
    pos_ref,
    vel_ref,
    acc_ref,
    jerk_ref,
    mass_ref,
    dt_ref,
    list_ref,
    count_ref,
    out_ref,
    pos_in,
    vel_in,
    acc_in,
    jerk_in,
    mass_in,
    dt_in,
    list_in,
    exact,
    feature,
    cross,
    wide,
    near,
    lists,
    rows,
    res,
    part,
    tiles,
    strip,
    a_send,
    a_recv,
    b_send,
    b_recv,
    r_send,
    r_recv,
    p_send,
    p_recv,
    f_send,
    f_recv,
    g_send,
    g_recv,
    in_sem,
):
    n_blk, low, n_far, n_near, total_stars = dims
    high = n_blk // low
    stars = mass_ref.shape[1]
    n_group = n_far * n_near
    b = lax.axis_index("blk")
    g = lax.axis_index("group")
    far = g // n_near
    close = lax.rem(g, n_near)

    def far_peer(step):
        return lax.rem(far + step, n_far)

    def near_peer(step):
        return lax.rem(close + step, n_near)

    early = max(1, low // 2)
    row, column = b // low, lax.rem(b, low)
    other = lax.rem(row + 1, high)

    def peer_at(place):
        if isinstance(place, int):
            spot = place if place < early else place - (early if place < early + low else low)
            rank = spot if spot < 3 else low + 2 - spot
            turn = (rank + 1) // 2 if rank % 2 else (low - rank // 2) % low
            return lax.rem(column + turn, low)
        spot = jnp.where(place < early + low, place - early, place - low)
        spot = jnp.where(place < early, place, spot)
        rank = jnp.where(spot < 3, spot, low + 2 - spot)
        turn = jnp.where(lax.rem(rank, 2) == 1, (rank + 1) // 2, lax.rem(low - rank // 2, low))
        return lax.rem(column + turn, low)

    fetch = [
        pltpu.make_async_copy(source, target, in_sem.at[place])
        for place, (source, target) in enumerate(
            [
                (pos_ref, pos_in),
                (vel_ref, vel_in),
                (acc_ref, acc_in),
                (jerk_ref, jerk_in),
                (mass_ref, mass_in),
                (dt_ref, dt_in),
                (list_ref, list_in),
            ]
        )
    ]
    for copy in fetch:
        copy.start()

    barrier = pltpu.get_barrier_semaphore()
    for step in range(1, n_far):
        pl.semaphore_signal(
            barrier, 1, device_id={"group": far_peer(step) * n_near + close}, device_id_type=MESH
        )
    for step in range(1, n_near):
        pl.semaphore_signal(
            barrier, 1, device_id={"group": far * n_near + near_peer(step)}, device_id_type=MESH
        )
    for step in range(1, low):
        side = row * low + lax.rem(column + step, low)
        pl.semaphore_signal(barrier, 1, device_id={"blk": side}, device_id_type=MESH)
    pl.semaphore_signal(barrier, 1, device_id={"blk": other * low + column}, device_id_type=MESH)

    fetch[6].wait()
    count = count_ref[0, 0]
    lane = lax.broadcasted_iota(jnp.int32, (1, LANES), 1)
    near[far] = jnp.where(lane < count, list_in[...], -1)

    pl.semaphore_wait(barrier, (n_far - 1) + (n_near - 1) + low)

    def a_copy(step, origin):
        return pltpu.make_async_remote_copy(
            src_ref=near.at[origin],
            dst_ref=near.at[origin],
            send_sem=a_send.at[step],
            recv_sem=a_recv.at[step],
            device_id={"group": far_peer(step) * n_near + close},
            device_id_type=MESH,
        )

    def b_copy(step, origin):
        return pltpu.make_async_remote_copy(
            src_ref=near,
            dst_ref=lists.at[origin],
            send_sem=b_send.at[step],
            recv_sem=b_recv.at[step],
            device_id={"group": far * n_near + near_peer(step)},
            device_id_type=MESH,
        )

    for step in range(1, n_far):
        a_copy(step, far).start()

    for copy in fetch[:6]:
        copy.wait()

    width = min(1024, stars)

    def predict(index, carry):
        here = pl.ds(pl.multiple_of(index * width, width), width)
        step = dt_in[:, here]
        vel, acc, jerk = vel_in[:, here], acc_in[:, here], jerk_in[:, here]
        ppos = pos_in[:, here] + step * (vel + step * (0.5 * acc + step * (jerk / 6.0)))
        pvel = vel + step * (acc + step * (0.5 * jerk))
        weight = mass_in[:, here] / total_stars
        blank = jnp.zeros_like(weight)
        for row in range(3):
            wide[row, :, here] = jnp.broadcast_to(ppos[row : row + 1], (8, width))
        state = jnp.concatenate([ppos, pvel, blank, blank], axis=0)
        eight = jnp.zeros_like(state)
        exact[:, here] = jnp.concatenate([*split(state), eight], axis=0).astype(jnp.bfloat16)
        scaled = jnp.concatenate([ppos * weight, pvel * weight, weight, blank], axis=0)
        feature[:, here] = jnp.concatenate([*split(scaled), eight], axis=0).astype(jnp.bfloat16)
        inner = jnp.sum(ppos * pvel, axis=0, keepdims=True)
        mixed = jnp.concatenate([ppos, pvel, inner, blank + 1.0], axis=0) * weight
        big, mid, small = split(mixed)
        cross[:, here] = jnp.concatenate([big, mid, big, mid, small, big], axis=0).astype(
            jnp.bfloat16
        )
        return carry

    lax.fori_loop(0, stars // width, predict, 0)

    for step in range(1, n_far):
        a_copy(step, lax.rem(far + n_far - step, n_far)).wait_recv()
    for step in range(1, n_near):
        b_copy(step, close).start()
    lists[close] = near[...]
    for step in range(1, n_near):
        b_copy(step, lax.rem(close + n_near - step, n_near)).wait_recv()

    entry = lists[...].reshape(n_group, LANES)
    valid = entry >= 0
    validf = jnp.where(valid, 1.0, 0.0).astype(jnp.float32)
    entryf = entry.astype(jnp.float32)
    r_iota = lax.broadcasted_iota(jnp.int32, (n_group, n_group), 0)
    c_iota = lax.broadcasted_iota(jnp.int32, (n_group, n_group), 1)
    before = jnp.where(c_iota < r_iota, 1.0, 0.0).astype(jnp.float32)
    starts = jnp.sum(
        jnp.dot(before, validf, preferred_element_type=jnp.float32), axis=1, keepdims=True
    )
    slot = lax.broadcasted_iota(jnp.int32, (n_group, LANES), 1).astype(jnp.float32)
    base = (g * ROWS).astype(jnp.float32)
    place = jnp.where(valid, starts + slot - base, -1.0)
    mine = close * n_far + far
    owner_row = lax.broadcasted_iota(jnp.int32, (n_group, LANES), 0)
    my_start = jnp.sum(
        jnp.sum(jnp.where(owner_row < mine, validf, 0.0), axis=1, keepdims=True),
        axis=0,
        keepdims=True,
    )
    found = jnp.concatenate(
        [
            jnp.sum(jnp.where(place == float(s), entryf, 0.0), axis=0, keepdims=True)
            for s in range(ROWS)
        ],
        axis=0,
    )
    chosen = jnp.sum(found, axis=1, keepdims=True).astype(jnp.int32)
    star_no = lax.broadcasted_iota(jnp.int32, (ROWS, width), 1)

    def gather(index, total):
        here = pl.ds(pl.multiple_of(index * width, width), width)
        hot = jnp.where(star_no + index * width == chosen, 1.0, 0.0).astype(jnp.bfloat16)
        return total + dot(exact[:, here], hot, True)

    picked = lax.fori_loop(
        0, stars // width, gather, jnp.zeros((32, ROWS), jnp.float32), unroll=True
    )
    picked = (picked[0:8] + picked[8:16]) + picked[16:24]
    rows[b] = jnp.concatenate([picked, jnp.zeros((8, LANES - ROWS), jnp.float32)], axis=1)

    def r_copy(peer, origin, mark):
        return pltpu.make_async_remote_copy(
            src_ref=rows.at[origin],
            dst_ref=rows.at[origin],
            send_sem=r_send.at[mark],
            recv_sem=r_recv.at[origin],
            device_id={"blk": peer},
            device_id_type=MESH,
        )

    def p_copy(peer, source, slot):
        return pltpu.make_async_remote_copy(
            src_ref=res.at[source],
            dst_ref=part.at[slot],
            send_sem=p_send.at[source],
            recv_sem=p_recv.at[slot],
            device_id={"blk": peer},
            device_id_type=MESH,
        )

    partner = other * low + column
    sum_copy = pltpu.make_async_remote_copy(
        src_ref=res.at[partner],
        dst_ref=part.at[n_blk],
        send_sem=p_send.at[partner],
        recv_sem=p_recv.at[n_blk],
        device_id={"blk": partner},
        device_id_type=MESH,
    )

    def side(step):
        return lax.rem(column + step, low)

    r_copy(partner, b, partner).start()
    for place in list(range(1, early)) + list(range(early + low, n_blk)):
        peer = row * low + peer_at(place)
        r_copy(peer, b, peer).start()

    def chunk(own, height, span):
        own_pos, own_vel = own[0:3], own[3:6]
        inner = jnp.sum(own_pos * own_vel, axis=0, keepdims=True)
        mixed = jnp.concatenate([-own_vel, -own_pos, jnp.ones_like(inner), inner], axis=0)
        big, mid, small = split(mixed)
        fill = jnp.zeros((LANES - 56, LANES), jnp.float32)
        down = jnp.transpose(
            jnp.concatenate([big, big, mid, mid, big, small, own, fill], axis=0)
        )
        mine_mixed = down[0:height, 0:48].astype(jnp.bfloat16)
        across = [
            jnp.broadcast_to(down[0:height, 48 + c : 49 + c], (height, LANES)) for c in range(3)
        ]

        def advance(tile, carried):
            sums, sx, sy, sz = carried
            base = pl.multiple_of(tile * span, span)
            here = pl.ds(base, span)
            turning = dot(mine_mixed, cross[:, here])
            tops, rests = [], []
            for part_at in range(0, span, LANES):
                at = pl.ds(pl.multiple_of(base + part_at, LANES), LANES)
                rx, ry, rz = (
                    jnp.concatenate([wide[c, :, at]] * (height // 8), axis=0) - across[c]
                    for c in range(3)
                )
                inverse = lax.rsqrt((rx * rx + ry * ry) + (rz * rz + soften))
                square = inverse * inverse
                cube = inverse * square
                swing = (turning[:, part_at : part_at + LANES] * square) * cube
                sx, sy, sz = sx + swing * rx, sy + swing * ry, sz + swing * rz
                top = cube.astype(jnp.bfloat16)
                tops.append(top)
                rests.append((cube - top.astype(jnp.float32)).astype(jnp.bfloat16))
            product = dot(jnp.concatenate(tops, axis=1), feature[:, here], True) + dot(
                jnp.concatenate(rests, axis=1), feature[:, here], True
            )
            return sums + product, sx, sy, sz

        zero = jnp.zeros((height, LANES), jnp.float32)
        sums, sx, sy, sz = lax.fori_loop(
            0,
            stars // span,
            advance,
            (jnp.zeros((height, 32), jnp.float32), zero, zero, zero),
            unroll=True,
        )
        out_lane = lax.broadcasted_iota(jnp.int32, (height, LANES), 1)
        piece = jnp.concatenate([sums, jnp.zeros((height, LANES - 32), jnp.float32)], axis=1)
        for c, total in enumerate((sx, sy, sz)):
            piece = jnp.where(out_lane == 32 + c, jnp.sum(total, axis=1, keepdims=True), piece)
        up = jnp.transpose(
            jnp.concatenate([piece, jnp.zeros((LANES - height, LANES), jnp.float32)], axis=0)
        )
        moment = (up[0:8] + up[8:16]) + up[16:24]
        weighed = moment[6:7]
        accel = moment[0:3] - own_pos * weighed
        jerks = (moment[3:6] - own_vel * weighed) - 3.0 * up[32:35]
        return jnp.concatenate([accel, jerks, jnp.zeros((2, LANES), jnp.float32)], axis=0)

    def half_of(place):
        return jnp.where((place >= early) & (place < early + low), other, row)

    def collect(place):
        peer = half_of(place) * low + peer_at(place)

        @pl.when(place != early)
        def _():
            r_copy(peer, peer, peer).wait_recv()

        return rows[peer]

    def deliver(place, result):
        line, half = peer_at(place), half_of(place)
        peer = half * low + line

        @pl.when(place == early)
        def _():
            part[partner] = result

        @pl.when(place != early)
        def _():
            res[peer] = result
            p_copy(row * low + line, peer, half * low + column).start()

    relay_at = min(3, early)

    def pairs(index, carry):
        first = 2 * index - 1

        @pl.when(first == relay_at)
        def _():
            r_copy(partner, partner, partner).wait_recv()

        def relay(step, carry):
            r_copy(row * low + side(step), partner, other * low + side(step)).start()
            return carry

        lax.fori_loop(1, jnp.where(first == relay_at, low, 1), relay, 0)
        own = collect(first) + pltpu.roll(collect(first + 1), ROWS, 1)
        result = chunk(own, 2 * ROWS, min(1024, stars))
        deliver(first, result)
        deliver(first + 1, pltpu.roll(result, LANES - ROWS, 1))
        return carry

    part[b] = chunk(rows[b], ROWS, min(2048, stars))
    lax.fori_loop(1, n_blk // 2, pairs, 0)
    for step in range(1, low):
        slot = other * low + side(low - step)
        p_copy(b, slot, slot).wait_recv()
    res[partner] = jnp.sum(part[pl.ds(other * low, low)], axis=0)
    sum_copy.start()
    last = n_blk - 1
    line = peer_at(last)
    peer = row * low + line
    r_copy(peer, peer, peer).wait_recv()
    res[peer] = chunk(rows[peer], ROWS, min(2048, stars))
    p_copy(peer, peer, b).start()

    for step in range(1, low):
        slot = row * low + side(low - step)
        p_copy(b, slot, slot).wait_recv()
    sum_copy.wait_recv()
    force = jnp.sum(part[pl.ds(row * low, low)], axis=0) + part[n_blk]
    force = jnp.where(lane < ROWS, force, 0.0)

    per_tile = LANES // ROWS
    spread = force
    for turn in range(1, per_tile):
        spread = jnp.where(
            lax.rem(close, per_tile) == turn, pltpu.roll(force, turn * ROWS, 1), spread
        )
    tiles[close] = spread

    def f_copy(step, origin):
        return pltpu.make_async_remote_copy(
            src_ref=tiles.at[origin],
            dst_ref=tiles.at[origin],
            send_sem=f_send.at[step],
            recv_sem=f_recv.at[step],
            device_id={"group": far * n_near + near_peer(step)},
            device_id_type=MESH,
        )

    def g_copy(step, origin):
        return pltpu.make_async_remote_copy(
            src_ref=strip.at[origin],
            dst_ref=strip.at[origin],
            send_sem=g_send.at[step],
            recv_sem=g_recv.at[step],
            device_id={"group": far_peer(step) * n_near + close},
            device_id_type=MESH,
        )

    for step in range(1, n_near):
        f_copy(step, close).start()
    for step in range(1, n_near):
        f_copy(step, lax.rem(close + n_near - step, n_near)).wait_recv()
    n_strip = n_near // per_tile
    for t in range(n_strip):
        joined = tiles[per_tile * t]
        for i in range(1, per_tile):
            joined = joined + tiles[per_tile * t + i]
        strip[far, t] = joined
    for step in range(1, n_far):
        g_copy(step, far).start()
    for step in range(1, n_far):
        a_copy(step, far).wait_send()
    for step in range(1, n_near):
        b_copy(step, close).wait_send()
        f_copy(step, close).wait_send()
    r_copy(partner, b, partner).wait_send()
    sum_copy.wait_send()
    for step in range(1, low):
        near_mark, far_mark = row * low + side(step), other * low + side(step)
        r_copy(near_mark, b, near_mark).wait_send()
        r_copy(near_mark, partner, far_mark).wait_send()
        p_copy(near_mark, near_mark, b).wait_send()
        p_copy(near_mark, far_mark, partner).wait_send()
    for step in range(1, n_far):
        g_copy(step, lax.rem(far + n_far - step, n_far)).wait_recv()

    whole = my_start.astype(jnp.int32)
    tile_no, shift = whole // LANES, lax.rem(whole, LANES)
    left = jnp.zeros((8, LANES), jnp.float32)
    right = jnp.zeros((8, LANES), jnp.float32)
    for t in range(n_far * n_strip):
        value = strip[t // n_strip, t % n_strip]
        left = jnp.where(tile_no == t, value, left)
        if t > 0:
            right = jnp.where(tile_no == t - 1, value, right)
    window = jnp.concatenate([left, right], axis=1)
    bit = LANES // 2
    while bit:
        moved = pltpu.roll(window, 2 * LANES - bit, 1)
        window = jnp.where(lax.rem(shift // bit, 2) == 1, moved, window)
        bit //= 2
    out_ref[:, 0, :] = jnp.where(lane < count, window[0:6, 0:LANES], 0.0)

    for step in range(1, n_far):
        g_copy(step, far).wait_send()


def on_device(
    low,
    n_near,
    star_pos,
    star_vel,
    star_acc,
    star_jerk,
    star_mass,
    star_dt,
    active_list,
    active_count,
):
    n_blk, n_group = lax.axis_size("blk"), lax.axis_size("group")
    n_far = n_group // n_near
    stars = star_mass.shape[0]
    slots = active_list.shape[2]
    dims = (n_blk, low, n_far, n_near, stars * n_blk)
    vmem = pl.BlockSpec(memory_space=pltpu.VMEM)
    f32, i32, bf16 = jnp.float32, jnp.int32, jnp.bfloat16
    dma = pltpu.SemaphoreType.DMA
    out = pl.pallas_call(
        functools.partial(kernel, dims),
        out_shape=jax.ShapeDtypeStruct((6, 1, slots), f32),
        in_specs=[pl.BlockSpec(memory_space=pl.ANY)] * 7 + [pl.BlockSpec(memory_space=pltpu.SMEM)],
        out_specs=vmem,
        scratch_shapes=[
            *[pltpu.VMEM((3, stars), f32)] * 4,
            pltpu.VMEM((1, stars), f32),
            pltpu.VMEM((1, stars), f32),
            pltpu.VMEM((1, slots), i32),
            pltpu.VMEM((32, stars), bf16),
            pltpu.VMEM((32, stars), bf16),
            pltpu.VMEM((48, stars), bf16),
            pltpu.VMEM((3, 8, stars), f32),
            pltpu.VMEM((n_far, 1, LANES), i32),
            pltpu.VMEM((n_near, n_far, 1, LANES), i32),
            pltpu.VMEM((n_blk, 8, LANES), f32),
            pltpu.VMEM((n_blk, 8, LANES), f32),
            pltpu.VMEM((n_blk + 1, 8, LANES), f32),
            pltpu.VMEM((n_near, 8, LANES), f32),
            pltpu.VMEM((n_far, n_near * ROWS // LANES, 8, LANES), f32),
            dma((n_far,)),
            dma((n_far,)),
            dma((n_near,)),
            dma((n_near,)),
            dma((n_blk,)),
            dma((n_blk,)),
            dma((n_blk,)),
            dma((n_blk + 1,)),
            dma((n_near,)),
            dma((n_near,)),
            dma((n_far,)),
            dma((n_far,)),
            dma((7,)),
        ],
        compiler_params=pltpu.CompilerParams(collective_id=0, has_side_effects=True),
    )(
        star_pos,
        star_vel,
        star_acc,
        star_jerk,
        star_mass.reshape(1, stars),
        star_dt.reshape(1, stars),
        active_list.reshape(1, slots),
        active_count,
    )
    return out.reshape(1, 1, 6, slots)


def solution(mesh):
    n_blk, n_group = mesh.shape["blk"], mesh.shape["group"]
    low = n_blk // 2
    n_near = 8 if n_group % 8 == 0 and n_group > 8 else 4
    return jax.shard_map(
        functools.partial(on_device, low, n_near),
        mesh=mesh,
        in_specs=(
            P(None, "blk"),
            P(None, "blk"),
            P(None, "blk"),
            P(None, "blk"),
            P("blk"),
            P("blk"),
            P("blk", "group", None),
            P("blk", "group"),
        ),
        out_specs=P("blk", "group", None, None),
        check_vma=False,
    )
```

```python
import functools

import jax
import jax.numpy as jnp
from jax import lax
from jax.experimental import pallas as pl
from jax.experimental.pallas import tpu as pltpu
from jax.sharding import PartitionSpec as P

MESH = pl.DeviceIdType.MESH
soften = 0.01
ROWS = 32
LANES = 128


def split(value):
    high = value.astype(jnp.bfloat16).astype(jnp.float32)
    rest = value - high
    middle = rest.astype(jnp.bfloat16).astype(jnp.float32)
    return high, middle, (rest - middle).astype(jnp.bfloat16).astype(jnp.float32)


def dot(left, right, transposed=False):
    dims = (((1,), (1 if transposed else 0,)), ((), ()))
    return lax.dot_general(left, right, dims, preferred_element_type=jnp.float32)


def kernel(
    dims,
    pos_ref,
    vel_ref,
    acc_ref,
    jerk_ref,
    mass_ref,
    dt_ref,
    list_ref,
    count_ref,
    out_ref,
    pos_in,
    vel_in,
    acc_in,
    jerk_in,
    mass_in,
    dt_in,
    list_in,
    exact,
    feature,
    cross,
    wide,
    near,
    lists,
    rows,
    res,
    part,
    tiles,
    strip,
    a_send,
    a_recv,
    b_send,
    b_recv,
    r_send,
    r_recv,
    p_send,
    p_recv,
    f_send,
    f_recv,
    g_send,
    g_recv,
    in_sem,
):
    n_blk, low, n_far, n_near, total_stars = dims
    high = n_blk // low
    stars = mass_ref.shape[1]
    n_group = n_far * n_near
    b = lax.axis_index("blk")
    g = lax.axis_index("group")
    far = g // n_near
    close = lax.rem(g, n_near)

    def far_peer(step):
        return lax.rem(far + step, n_far)

    def near_peer(step):
        return lax.rem(close + step, n_near)

    early = max(1, low // 2)
    row, column = b // low, lax.rem(b, low)
    other = lax.rem(row + 1, high)

    def peer_at(place):
        if isinstance(place, int):
            spot = place if place < early else place - (early if place < early + low else low)
            rank = spot if spot < 3 else low + 2 - spot
            turn = (rank + 1) // 2 if rank % 2 else (low - rank // 2) % low
            return lax.rem(column + turn, low)
        spot = jnp.where(place < early + low, place - early, place - low)
        spot = jnp.where(place < early, place, spot)
        rank = jnp.where(spot < 3, spot, low + 2 - spot)
        turn = jnp.where(lax.rem(rank, 2) == 1, (rank + 1) // 2, lax.rem(low - rank // 2, low))
        return lax.rem(column + turn, low)

    fetch = [
        pltpu.make_async_copy(source, target, in_sem.at[place])
        for place, (source, target) in enumerate(
            [
                (pos_ref, pos_in),
                (vel_ref, vel_in),
                (acc_ref, acc_in),
                (jerk_ref, jerk_in),
                (mass_ref, mass_in),
                (dt_ref, dt_in),
                (list_ref, list_in),
            ]
        )
    ]
    for copy in fetch:
        copy.start()

    barrier = pltpu.get_barrier_semaphore()
    for step in range(1, n_far):
        pl.semaphore_signal(
            barrier, 1, device_id={"group": far_peer(step) * n_near + close}, device_id_type=MESH
        )
    for step in range(1, n_near):
        pl.semaphore_signal(
            barrier, 1, device_id={"group": far * n_near + near_peer(step)}, device_id_type=MESH
        )
    for step in range(1, low):
        side = row * low + lax.rem(column + step, low)
        pl.semaphore_signal(barrier, 1, device_id={"blk": side}, device_id_type=MESH)
    pl.semaphore_signal(barrier, 1, device_id={"blk": other * low + column}, device_id_type=MESH)

    fetch[6].wait()
    count = count_ref[0, 0]
    lane = lax.broadcasted_iota(jnp.int32, (1, LANES), 1)
    near[far] = jnp.where(lane < count, list_in[...], -1)

    pl.semaphore_wait(barrier, (n_far - 1) + (n_near - 1) + low)

    def a_copy(step, origin):
        return pltpu.make_async_remote_copy(
            src_ref=near.at[origin],
            dst_ref=near.at[origin],
            send_sem=a_send.at[step],
            recv_sem=a_recv.at[step],
            device_id={"group": far_peer(step) * n_near + close},
            device_id_type=MESH,
        )

    def b_copy(step, origin):
        return pltpu.make_async_remote_copy(
            src_ref=near,
            dst_ref=lists.at[origin],
            send_sem=b_send.at[step],
            recv_sem=b_recv.at[step],
            device_id={"group": far * n_near + near_peer(step)},
            device_id_type=MESH,
        )

    for step in range(1, n_far):
        a_copy(step, far).start()

    for copy in fetch[:6]:
        copy.wait()

    width = min(1024, stars)

    def predict(index, carry):
        here = pl.ds(pl.multiple_of(index * width, width), width)
        step = dt_in[:, here]
        vel, acc, jerk = vel_in[:, here], acc_in[:, here], jerk_in[:, here]
        ppos = pos_in[:, here] + step * (vel + step * (0.5 * acc + step * (jerk / 6.0)))
        pvel = vel + step * (acc + step * (0.5 * jerk))
        weight = mass_in[:, here] / total_stars
        blank = jnp.zeros_like(weight)
        for row in range(3):
            wide[row, :, here] = jnp.broadcast_to(ppos[row : row + 1], (8, width))
        state = jnp.concatenate([ppos, pvel, blank, blank], axis=0)
        eight = jnp.zeros_like(state)
        exact[:, here] = jnp.concatenate([*split(state), eight], axis=0).astype(jnp.bfloat16)
        scaled = jnp.concatenate([ppos * weight, pvel * weight, weight, blank], axis=0)
        feature[:, here] = jnp.concatenate([*split(scaled), eight], axis=0).astype(jnp.bfloat16)
        inner = jnp.sum(ppos * pvel, axis=0, keepdims=True)
        mixed = jnp.concatenate([ppos, pvel, inner, blank + 1.0], axis=0) * weight
        big, mid, small = split(mixed)
        cross[:, here] = jnp.concatenate([big, mid, big, mid, small, big], axis=0).astype(
            jnp.bfloat16
        )
        return carry

    lax.fori_loop(0, stars // width, predict, 0)

    for step in range(1, n_far):
        a_copy(step, lax.rem(far + n_far - step, n_far)).wait_recv()
    for step in range(1, n_near):
        b_copy(step, close).start()
    lists[close] = near[...]
    for step in range(1, n_near):
        b_copy(step, lax.rem(close + n_near - step, n_near)).wait_recv()

    entry = lists[...].reshape(n_group, LANES)
    valid = entry >= 0
    validf = jnp.where(valid, 1.0, 0.0).astype(jnp.float32)
    entryf = entry.astype(jnp.float32)
    r_iota = lax.broadcasted_iota(jnp.int32, (n_group, n_group), 0)
    c_iota = lax.broadcasted_iota(jnp.int32, (n_group, n_group), 1)
    before = jnp.where(c_iota < r_iota, 1.0, 0.0).astype(jnp.float32)
    starts = jnp.sum(
        jnp.dot(before, validf, preferred_element_type=jnp.float32), axis=1, keepdims=True
    )
    slot = lax.broadcasted_iota(jnp.int32, (n_group, LANES), 1).astype(jnp.float32)
    base = (g * ROWS).astype(jnp.float32)
    place = jnp.where(valid, starts + slot - base, -1.0)
    mine = close * n_far + far
    owner_row = lax.broadcasted_iota(jnp.int32, (n_group, LANES), 0)
    my_start = jnp.sum(
        jnp.sum(jnp.where(owner_row < mine, validf, 0.0), axis=1, keepdims=True),
        axis=0,
        keepdims=True,
    )
    found = jnp.concatenate(
        [
            jnp.sum(jnp.where(place == float(s), entryf, 0.0), axis=0, keepdims=True)
            for s in range(ROWS)
        ],
        axis=0,
    )
    chosen = jnp.sum(found, axis=1, keepdims=True).astype(jnp.int32)
    star_no = lax.broadcasted_iota(jnp.int32, (ROWS, width), 1)

    def gather(index, total):
        here = pl.ds(pl.multiple_of(index * width, width), width)
        hot = jnp.where(star_no + index * width == chosen, 1.0, 0.0).astype(jnp.bfloat16)
        return total + dot(exact[:, here], hot, True)

    picked = lax.fori_loop(
        0, stars // width, gather, jnp.zeros((32, ROWS), jnp.float32), unroll=True
    )
    picked = (picked[0:8] + picked[8:16]) + picked[16:24]
    rows[b] = jnp.concatenate([picked, jnp.zeros((8, LANES - ROWS), jnp.float32)], axis=1)

    def r_copy(peer, origin, mark):
        return pltpu.make_async_remote_copy(
            src_ref=rows.at[origin],
            dst_ref=rows.at[origin],
            send_sem=r_send.at[mark],
            recv_sem=r_recv.at[origin],
            device_id={"blk": peer},
            device_id_type=MESH,
        )

    def p_copy(peer, source, slot):
        return pltpu.make_async_remote_copy(
            src_ref=res.at[source],
            dst_ref=part.at[slot],
            send_sem=p_send.at[source],
            recv_sem=p_recv.at[slot],
            device_id={"blk": peer},
            device_id_type=MESH,
        )

    partner = other * low + column
    sum_copy = pltpu.make_async_remote_copy(
        src_ref=res.at[partner],
        dst_ref=part.at[n_blk],
        send_sem=p_send.at[partner],
        recv_sem=p_recv.at[n_blk],
        device_id={"blk": partner},
        device_id_type=MESH,
    )

    def side(step):
        return lax.rem(column + step, low)

    r_copy(partner, b, partner).start()
    for place in list(range(1, early)) + list(range(early + low, n_blk)):
        peer = row * low + peer_at(place)
        r_copy(peer, b, peer).start()

    def chunk(own, height, span):
        own_pos, own_vel = own[0:3], own[3:6]
        inner = jnp.sum(own_pos * own_vel, axis=0, keepdims=True)
        mixed = jnp.concatenate([-own_vel, -own_pos, jnp.ones_like(inner), inner], axis=0)
        big, mid, small = split(mixed)
        fill = jnp.zeros((LANES - 56, LANES), jnp.float32)
        down = jnp.transpose(
            jnp.concatenate([big, big, mid, mid, big, small, own, fill], axis=0)
        )
        mine_mixed = down[0:height, 0:48].astype(jnp.bfloat16)
        across = [
            jnp.broadcast_to(down[0:height, 48 + c : 49 + c], (height, LANES)) for c in range(3)
        ]

        def advance(tile, carried):
            sums, sx, sy, sz = carried
            base = pl.multiple_of(tile * span, span)
            here = pl.ds(base, span)
            turning = dot(mine_mixed, cross[:, here])
            tops, rests = [], []
            for part_at in range(0, span, LANES):
                at = pl.ds(pl.multiple_of(base + part_at, LANES), LANES)
                rx, ry, rz = (
                    jnp.concatenate([wide[c, :, at]] * (height // 8), axis=0) - across[c]
                    for c in range(3)
                )
                inverse = lax.rsqrt((rx * rx + ry * ry) + (rz * rz + soften))
                square = inverse * inverse
                cube = inverse * square
                swing = (turning[:, part_at : part_at + LANES] * square) * cube
                sx, sy, sz = sx + swing * rx, sy + swing * ry, sz + swing * rz
                top = cube.astype(jnp.bfloat16)
                tops.append(top)
                rests.append((cube - top.astype(jnp.float32)).astype(jnp.bfloat16))
            product = dot(jnp.concatenate(tops, axis=1), feature[:, here], True) + dot(
                jnp.concatenate(rests, axis=1), feature[:, here], True
            )
            return sums + product, sx, sy, sz

        zero = jnp.zeros((height, LANES), jnp.float32)
        sums, sx, sy, sz = lax.fori_loop(
            0,
            stars // span,
            advance,
            (jnp.zeros((height, 32), jnp.float32), zero, zero, zero),
            unroll=True,
        )
        out_lane = lax.broadcasted_iota(jnp.int32, (height, LANES), 1)
        piece = jnp.concatenate([sums, jnp.zeros((height, LANES - 32), jnp.float32)], axis=1)
        for c, total in enumerate((sx, sy, sz)):
            piece = jnp.where(out_lane == 32 + c, jnp.sum(total, axis=1, keepdims=True), piece)
        up = jnp.transpose(
            jnp.concatenate([piece, jnp.zeros((LANES - height, LANES), jnp.float32)], axis=0)
        )
        moment = (up[0:8] + up[8:16]) + up[16:24]
        weighed = moment[6:7]
        accel = moment[0:3] - own_pos * weighed
        jerks = (moment[3:6] - own_vel * weighed) - 3.0 * up[32:35]
        return jnp.concatenate([accel, jerks, jnp.zeros((2, LANES), jnp.float32)], axis=0)

    def half_of(place):
        return jnp.where((place >= early) & (place < early + low), other, row)

    def collect(place):
        peer = half_of(place) * low + peer_at(place)

        @pl.when(place != early)
        def _():
            r_copy(peer, peer, peer).wait_recv()

        return rows[peer]

    def deliver(place, result):
        line, half = peer_at(place), half_of(place)
        peer = half * low + line

        @pl.when(place == early)
        def _():
            part[partner] = result

        @pl.when(place != early)
        def _():
            res[peer] = result
            p_copy(row * low + line, peer, half * low + column).start()

    relay_at = min(3, early)

    def pairs(index, carry):
        first = 2 * index - 1

        @pl.when(first == relay_at)
        def _():
            r_copy(partner, partner, partner).wait_recv()

        def relay(step, carry):
            r_copy(row * low + side(step), partner, other * low + side(step)).start()
            return carry

        lax.fori_loop(1, jnp.where(first == relay_at, low, 1), relay, 0)
        own = collect(first) + pltpu.roll(collect(first + 1), ROWS, 1)
        result = chunk(own, 2 * ROWS, min(1024, stars))
        deliver(first, result)
        deliver(first + 1, pltpu.roll(result, LANES - ROWS, 1))
        return carry

    lax.fori_loop(1, n_blk // 2, pairs, 0)
    for step in range(1, low):
        slot = other * low + side(low - step)
        p_copy(b, slot, slot).wait_recv()
    res[partner] = jnp.sum(part[pl.ds(other * low, low)], axis=0)
    sum_copy.start()
    last = n_blk - 1
    line = peer_at(last)
    peer = row * low + line
    r_copy(peer, peer, peer).wait_recv()
    res[peer] = chunk(rows[peer], ROWS, min(2048, stars))
    p_copy(peer, peer, b).start()
    part[b] = chunk(rows[b], ROWS, min(2048, stars))

    for step in range(1, low):
        slot = row * low + side(low - step)
        p_copy(b, slot, slot).wait_recv()
    sum_copy.wait_recv()
    force = jnp.sum(part[pl.ds(row * low, low)], axis=0) + part[n_blk]
    force = jnp.where(lane < ROWS, force, 0.0)

    per_tile = LANES // ROWS
    spread = force
    for turn in range(1, per_tile):
        spread = jnp.where(
            lax.rem(close, per_tile) == turn, pltpu.roll(force, turn * ROWS, 1), spread
        )
    tiles[close] = spread

    def f_copy(step, origin):
        return pltpu.make_async_remote_copy(
            src_ref=tiles.at[origin],
            dst_ref=tiles.at[origin],
            send_sem=f_send.at[step],
            recv_sem=f_recv.at[step],
            device_id={"group": far * n_near + near_peer(step)},
            device_id_type=MESH,
        )

    def g_copy(step, origin):
        return pltpu.make_async_remote_copy(
            src_ref=strip.at[origin],
            dst_ref=strip.at[origin],
            send_sem=g_send.at[step],
            recv_sem=g_recv.at[step],
            device_id={"group": far_peer(step) * n_near + close},
            device_id_type=MESH,
        )

    for step in range(1, n_near):
        f_copy(step, close).start()
    for step in range(1, n_near):
        f_copy(step, lax.rem(close + n_near - step, n_near)).wait_recv()
    n_strip = n_near // per_tile
    for t in range(n_strip):
        joined = tiles[per_tile * t]
        for i in range(1, per_tile):
            joined = joined + tiles[per_tile * t + i]
        strip[far, t] = joined
    for step in range(1, n_far):
        g_copy(step, far).start()
    for step in range(1, n_far):
        a_copy(step, far).wait_send()
    for step in range(1, n_near):
        b_copy(step, close).wait_send()
        f_copy(step, close).wait_send()
    r_copy(partner, b, partner).wait_send()
    sum_copy.wait_send()
    for step in range(1, low):
        near_mark, far_mark = row * low + side(step), other * low + side(step)
        r_copy(near_mark, b, near_mark).wait_send()
        r_copy(near_mark, partner, far_mark).wait_send()
        p_copy(near_mark, near_mark, b).wait_send()
        p_copy(near_mark, far_mark, partner).wait_send()
    for step in range(1, n_far):
        g_copy(step, lax.rem(far + n_far - step, n_far)).wait_recv()

    whole = my_start.astype(jnp.int32)
    tile_no, shift = whole // LANES, lax.rem(whole, LANES)
    left = jnp.zeros((8, LANES), jnp.float32)
    right = jnp.zeros((8, LANES), jnp.float32)
    for t in range(n_far * n_strip):
        value = strip[t // n_strip, t % n_strip]
        left = jnp.where(tile_no == t, value, left)
        if t > 0:
            right = jnp.where(tile_no == t - 1, value, right)
    window = jnp.concatenate([left, right], axis=1)
    bit = LANES // 2
    while bit:
        moved = pltpu.roll(window, 2 * LANES - bit, 1)
        window = jnp.where(lax.rem(shift // bit, 2) == 1, moved, window)
        bit //= 2
    out_ref[:, 0, :] = jnp.where(lane < count, window[0:6, 0:LANES], 0.0)

    for step in range(1, n_far):
        g_copy(step, far).wait_send()


def on_device(
    low,
    n_near,
    star_pos,
    star_vel,
    star_acc,
    star_jerk,
    star_mass,
    star_dt,
    active_list,
    active_count,
):
    n_blk, n_group = lax.axis_size("blk"), lax.axis_size("group")
    n_far = n_group // n_near
    stars = star_mass.shape[0]
    slots = active_list.shape[2]
    dims = (n_blk, low, n_far, n_near, stars * n_blk)
    vmem = pl.BlockSpec(memory_space=pltpu.VMEM)
    f32, i32, bf16 = jnp.float32, jnp.int32, jnp.bfloat16
    dma = pltpu.SemaphoreType.DMA
    out = pl.pallas_call(
        functools.partial(kernel, dims),
        out_shape=jax.ShapeDtypeStruct((6, 1, slots), f32),
        in_specs=[pl.BlockSpec(memory_space=pl.ANY)] * 7 + [pl.BlockSpec(memory_space=pltpu.SMEM)],
        out_specs=vmem,
        scratch_shapes=[
            *[pltpu.VMEM((3, stars), f32)] * 4,
            pltpu.VMEM((1, stars), f32),
            pltpu.VMEM((1, stars), f32),
            pltpu.VMEM((1, slots), i32),
            pltpu.VMEM((32, stars), bf16),
            pltpu.VMEM((32, stars), bf16),
            pltpu.VMEM((48, stars), bf16),
            pltpu.VMEM((3, 8, stars), f32),
            pltpu.VMEM((n_far, 1, LANES), i32),
            pltpu.VMEM((n_near, n_far, 1, LANES), i32),
            pltpu.VMEM((n_blk, 8, LANES), f32),
            pltpu.VMEM((n_blk, 8, LANES), f32),
            pltpu.VMEM((n_blk + 1, 8, LANES), f32),
            pltpu.VMEM((n_near, 8, LANES), f32),
            pltpu.VMEM((n_far, n_near * ROWS // LANES, 8, LANES), f32),
            dma((n_far,)),
            dma((n_far,)),
            dma((n_near,)),
            dma((n_near,)),
            dma((n_blk,)),
            dma((n_blk,)),
            dma((n_blk,)),
            dma((n_blk + 1,)),
            dma((n_near,)),
            dma((n_near,)),
            dma((n_far,)),
            dma((n_far,)),
            dma((7,)),
        ],
        compiler_params=pltpu.CompilerParams(collective_id=0, has_side_effects=True),
    )(
        star_pos,
        star_vel,
        star_acc,
        star_jerk,
        star_mass.reshape(1, stars),
        star_dt.reshape(1, stars),
        active_list.reshape(1, slots),
        active_count,
    )
    return out.reshape(1, 1, 6, slots)


def solution(mesh):
    n_blk, n_group = mesh.shape["blk"], mesh.shape["group"]
    low = n_blk // 2
    n_near = 8 if n_group % 8 == 0 and n_group > 8 else 4
    return jax.shard_map(
        functools.partial(on_device, low, n_near),
        mesh=mesh,
        in_specs=(
            P(None, "blk"),
            P(None, "blk"),
            P(None, "blk"),
            P(None, "blk"),
            P("blk"),
            P("blk"),
            P("blk", "group", None),
            P("blk", "group"),
        ),
        out_specs=P("blk", "group", None, None),
        check_vma=False,
    )
```
